32 devices in a mesh: wide: 8 (over y, x, core), narrow: 4 (over z).
Axes of the slice: x: 2, y: 2, z: 4, core: 2. Of those that a mesh axis runs over, the one named last changes fastest.
Arguments:
- pooled: bfloat16 [16384, 1024], P(('wide', 'narrow')), may hold values from -6 to 6
- cotangent: bfloat16 [16384, 512], P(('wide', 'narrow')), may hold values from -6 to 6
- w_first: bfloat16 [1024, 1024], P('narrow'), may hold values from -0.1875 to 0.1875
- b_first: float32 [1024], replicated, may hold values from -5 to 5
- w_second: bfloat16 [1024, 512], P('narrow'), may hold values from -0.1875 to 0.1875
- counts: bfloat16 [8, 64, 16384], P(None, 'narrow', 'wide'), may hold values from 0 to 3, as said below
- row_ids: int32 [8, 64], P(None, 'narrow'), may hold values from 0 to 63, as said below
- table: float32 [8, 256, 128], P(None, 'narrow'), may hold values from -6 to 6
- accum: float32 [8, 256, 128], P(None, 'narrow'), may hold values from 0.1 to 10
Outputs:
- new_table: float32 [8, 256, 128], P(None, 'narrow')
- new_accum: float32 [8, 256, 128], P(None, 'narrow')
The draws below stay inside these ranges and needn't reach their ends.
Inputs may be any that keep to these rules, and one draw needn't show every extreme that they name: `counts`: each entry is zero where the sample does not look up the active row, else a positive lookup weight. `row_ids`: for each table, the 16 ids of one owner (slots j * 16 to (j + 1) * 16 - 1) are distinct.
All inputs are finite; a program needn't handle non-finite values.
Results may differ from the reference program's by a relative error of at most 0.0038.
Values may be sent and summed in bfloat16 or wider, within the bound.
A program may use at most 128 MiB of HBM per device.

```python
import math
import jax
import jax.numpy as jnp
from jax import lax

TABLES = 8
EMB = 128
INNER = 1024
TOP = 512
ACT = 16
ROWS_DEV = 64
EMB_ALL = 1024
GROUP_BAGS = 2048
SAMPLES = 16384
N_WIDE = 8
N_NARROW = 4


def draw_counts(key, part):
    level_key = jax.random.fold_in(key, 11)
    hit_key = jax.random.fold_in(key, 12)
    value_key = jax.random.fold_in(key, 13)
    shape = (TABLES, N_NARROW * ACT, N_WIDE * GROUP_BAGS)
    levels = jax.random.randint(level_key, (TABLES, N_NARROW * ACT, 1), 0, 4)
    limits = jnp.right_shift(jnp.int32(1024), levels.astype(jnp.int32))
    hits = jax.random.randint(hit_key, shape, 0, 1024) < limits
    values = 0.25 + 2.75 * jax.random.uniform(value_key, shape, jnp.float32)
    return jnp.where(hits, values, jnp.float32(0.0)).astype(jnp.bfloat16)


def pick_rows(subkey):
    return jax.random.permutation(subkey, ROWS_DEV)[:ACT]


def draw_row_ids(key, part):
    keys = jax.random.split(jax.random.fold_in(key, 21), TABLES * N_NARROW)
    picks = jax.vmap(pick_rows)(keys)
    return picks.reshape(TABLES, N_NARROW * ACT).astype(jnp.int32)


def shard_levels(key, shape, pieces, least, high):
    level = 1.0
    for axis_at, blocks in pieces:
        steps = jax.random.uniform(jax.random.fold_in(jax.random.fold_in(key, 6), axis_at), (blocks,), jnp.float32, least / len(pieces), high / len(pieces))
        level = level * jnp.repeat(jnp.exp(steps), shape[axis_at] // blocks).reshape((-1,) + (1,) * (len(shape) - 1 - axis_at))
    return level


def normal_values(rng, extent, scale, bound, shards=(), kind=jnp.bfloat16):
    gain = shard_levels(rng, extent, shards, -0.22, 0.18) if shards else 1.0
    array = jax.random.normal(rng, extent, jnp.float32) * scale * gain
    return jnp.minimum(jnp.maximum(array, -bound), bound).astype(kind)


def setup_inputs(seed: int = 0) -> dict:
    streams_of = jax.random.split(jax.random.key(seed), 10)
    pooled = normal_values(streams_of[0], (SAMPLES, EMB_ALL), 1.0, 6.0, ((0, 32),))
    cotangent = normal_values(streams_of[1], (SAMPLES, TOP), 1.0, 6.0, ((0, 32),))
    w_first = normal_values(streams_of[2], (EMB_ALL, INNER), EMB_ALL ** -0.5, 0.1875, ((0, 4),))
    b_first = normal_values(streams_of[3], (INNER,), 1.0, 5.0, (), jnp.float32)
    w_second = normal_values(streams_of[4], (INNER, TOP), INNER ** -0.5, 0.1875, ((0, 4),))
    counts = draw_counts(jax.random.fold_in(streams_of[9], 71), 0)
    row_ids = draw_row_ids(jax.random.fold_in(streams_of[9], 71), 0)
    table = normal_values(streams_of[7], (TABLES, N_NARROW * ROWS_DEV, EMB), 1.0, 6.0, ((1, 4),), jnp.float32)
    accum = jnp.clip(jnp.exp(math.log(10.0) - 4.6051702 * jax.random.uniform(streams_of[8], (TABLES, N_NARROW * ROWS_DEV, EMB), jnp.float32) ** shard_levels(streams_of[8], (TABLES, N_NARROW * ROWS_DEV, EMB), ((1, 4),), -0.2, 0.2)), 0.1, 10.0)
    return dict(pooled=pooled, cotangent=cotangent, w_first=w_first, b_first=b_first, w_second=w_second, counts=counts, row_ids=row_ids, table=table, accum=accum)


clip_factor = 0.5
learn_rate = 0.05
epsilon = 1e-08

def tower_back(inputs, cotangent, w_first, b_first, w_second):
    hidden_in = jnp.dot(inputs, w_first, preferred_element_type=jnp.float32) + b_first
    back_hidden = lax.dot_general(cotangent, w_second, (((1,), (1,)), ((), ())), preferred_element_type=jnp.float32)
    sigmoid_val = jax.nn.sigmoid(hidden_in)
    slopes = sigmoid_val * (1.0 + hidden_in * (1.0 - sigmoid_val))
    deltas = (back_hidden * slopes).astype(jnp.bfloat16)
    return lax.dot_general(deltas, w_first, (((1,), (1,)), ((), ())), preferred_element_type=jnp.float32).astype(jnp.bfloat16)

def clip_rows(grads, limit):
    norms = jnp.sqrt(lax.optimization_barrier(jnp.sum(grads * grads, axis=-1, keepdims=True)))
    return grads * (limit / jnp.maximum(norms, limit))

def reference(pooled, cotangent, w_first, b_first, w_second, counts, row_ids, table, accum):
    tables = counts.shape[0]
    emb = table.shape[2]
    bags = counts.shape[2] // N_WIDE
    scale = 1.0 / math.sqrt(bags)
    limit = clip_factor * math.sqrt(emb)

    def one_group(group_index):
        offset = group_index * bags
        inputs = lax.dynamic_slice_in_dim(pooled, offset, bags, 0)
        upstream = lax.dynamic_slice_in_dim(cotangent, offset, bags, 0)
        grad_in = tower_back(inputs, upstream, w_first, b_first, w_second)
        lookups = lax.dynamic_slice_in_dim(counts, offset, bags, 2)
        grads = jnp.stack([jnp.dot(lookups[table_no], grad_in[:, table_no * emb:(table_no + 1) * emb], preferred_element_type=jnp.float32) for table_no in range(tables)])
        return clip_rows(grads * scale, limit)
    summed = lax.optimization_barrier(jnp.sum(lax.map(one_group, jnp.arange(N_WIDE, dtype=jnp.int32)), axis=0))
    slots = row_ids.shape[1]
    owners = jnp.arange(slots, dtype=jnp.int32) // ACT
    rows_global = (owners * ROWS_DEV)[None, :] + row_ids
    table_index = jnp.arange(tables, dtype=jnp.int32)[:, None]
    current = table[table_index, rows_global]
    old_acc = accum[table_index, rows_global]
    new_acc = old_acc + summed * summed
    new_rows = current - learn_rate * summed / (jnp.sqrt(new_acc) + epsilon)
    new_table = table.at[table_index, rows_global].set(new_rows)
    new_accum = accum.at[table_index, rows_global].set(new_acc)
    return (new_table, new_accum)
```

```python
import functools
import math

import jax
import jax.numpy as jnp
from jax import lax
from jax.experimental import pallas as pl
from jax.experimental.pallas import tpu as pltpu
from jax.sharding import PartitionSpec as P

MESH = pl.DeviceIdType.MESH
clip_factor = 0.5
learn_rate = 0.05
epsilon = 1e-08
skew = 3
NT = (((1,), (1,)), ((), ()))


def flip(index, bit):
    return index + bit * (1 - 2 * ((index // bit) % 2))


def pieces_of(shard_rows, n_wide):
    pieces = 1
    while n_wide % (2 * pieces) == 0 and shard_rows % (32 * pieces) == 0:
        pieces *= 2
    return pieces


def masks_of(pieces):
    across = list(range(2, pieces, 2))
    return [masks for masks in (across, [1] if pieces > 1 else []) if masks]


def flips(index, mask):
    bit = 1
    while bit <= mask:
        if mask & bit:
            index = flip(index, bit)
        bit *= 2
    return index


def tower_kernel(
    n_wide, n_narrow, pieces, scale, limit,
    pooled_hbm, cot_hbm, w1_hbm, w2_hbm, bias_ref, counts_hbm, ids_ref, out_ref,
    pooled, cot, w1, w2, looks, hidden, back, deltas, gfull, gsend, grecv, sums,
    local_sem, send_sem, wrecv_sem, crecv_sem, grecv_sem, arecv_sem,
):
    wide = lax.axis_index("wide")
    narrow = lax.axis_index("narrow")
    shard = w1_hbm.shape[0]
    piece_rows = shard // pieces
    bags = pooled.shape[0]
    inner = w1.shape[1]
    emb = gfull.shape[3]
    tables, slots = looks.shape[1], looks.shape[2]
    rest = n_narrow - 1
    part = wide % pieces
    base = wide - part
    masks = masks_of(pieces)
    half = inner // 2
    units = [
        (w1, w1_hbm, pl.ds(0, half)),
        (w1, w1_hbm, pl.ds(half, half)),
        (w2, w2_hbm, pl.ds(0, w2.shape[1])),
    ]
    stages = len(masks)

    def lane_block(index, size):
        return pl.ds(pl.multiple_of(index * size, size), size)

    def local(step, src, dst):
        return pltpu.make_async_copy(src, dst, local_sem.at[step])

    own_rows = lane_block(narrow, shard)
    locals_ = [
        local(0, pooled_hbm, pooled),
        local(1, w1_hbm, w1.at[own_rows, :]),
        local(2, cot_hbm, cot),
        local(3, w2_hbm, w2.at[own_rows, :]),
        local(4, counts_hbm.at[:, :, lane_block(narrow, bags)], looks.at[narrow]),
    ]
    for copy in locals_:
        copy.start()

    barrier = pltpu.get_barrier_semaphore()
    for d in range(1, n_narrow):
        pl.semaphore_signal(
            barrier, inc=1, device_id={"narrow": (narrow + d) % n_narrow}, device_id_type=MESH
        )
    for d in range(1, n_wide):
        pl.semaphore_signal(
            barrier, inc=1, device_id={"wide": (wide + d) % n_wide}, device_id_type=MESH
        )
    pl.semaphore_wait(barrier, n_narrow + n_wide - 2)

    def remote(src, dst, send, recv, device):
        return pltpu.make_async_remote_copy(
            src_ref=src, dst_ref=dst, send_sem=send, recv_sem=recv,
            device_id=device, device_id_type=MESH,
        )

    sent = []

    def launch(copy):
        copy.start()
        sent.append(copy)

    def rows_at(source, piece):
        return pl.ds(pl.multiple_of(source * shard + piece * piece_rows, piece_rows), piece_rows)

    for d in range(rest):
        target = {"narrow": (narrow + d + 1) % n_narrow}
        for u, (ref, shard_ref, columns) in enumerate(units):
            launch(remote(
                shard_ref.at[lane_block(part, piece_rows), columns],
                ref.at[rows_at(narrow, part), columns],
                send_sem, wrecv_sem.at[u, d, 0], target,
            ))
    for d in range(rest):
        owner = (narrow + d + 1) % n_narrow
        launch(remote(
            counts_hbm.at[:, :, lane_block(owner, bags)], looks.at[narrow],
            send_sem, crecv_sem.at[d], {"narrow": owner},
        ))

    held = [[[part] for _ in range(rest)] for _ in units]

    def stage_arrive(u, d, stage):
        source = (narrow + n_narrow - d - 1) % n_narrow
        ref, _, columns = units[u]
        if stage == 0:
            moves = [(part, {"narrow": source})]
            first = 0
        else:
            moves = [
                (flips(q, mask), {"wide": base + flips(part, mask)})
                for mask in masks[stage - 1] for q in held[u][d]
            ]
            first = len(held[u][d])
        for i, (q, device) in enumerate(moves):
            view = ref.at[rows_at(source, q), columns]
            remote(
                view, view, send_sem, wrecv_sem.at[u, d, first + i], device
            ).wait_recv()
        if stage:
            held[u][d] = held[u][d] + [q for q, _ in moves]

    def stage_send(u, d, stage):
        source = (narrow + n_narrow - d - 1) % n_narrow
        ref, _, columns = units[u]
        slot = len(held[u][d])
        for mask in masks[stage]:
            for q in held[u][d]:
                view = ref.at[rows_at(source, q), columns]
                launch(remote(
                    view, view, send_sem, wrecv_sem.at[u, d, slot],
                    {"wide": base + flips(part, mask)},
                ))
                slot += 1

    tile = min(256, inner)

    def add_chunk(source, fresh):
        rows = lane_block(source, shard)
        lhs = pooled[:, rows]

        value = jnp.dot(lhs, w1[rows, :], preferred_element_type=jnp.float32)
        if fresh:
            hidden[...] = value
        else:
            hidden[...] = hidden[...] + value
        back[:, rows] = lax.dot_general(
            cot[...], w2[rows, :], NT, preferred_element_type=jnp.float32
        )

    chunked = shard % 128 == 0
    for copy in locals_:
        copy.wait()
    if chunked:
        add_chunk(narrow, True)
    items = rest * len(units)
    for t in range(items + skew * stages):
        for stage in range(stages + 1):
            item = t - skew * stage
            if 0 <= item < items:
                d, u = divmod(item, len(units))
                stage_arrive(u, d, stage)
                if stage < stages:
                    stage_send(u, d, stage)
                elif chunked and u == len(units) - 1:
                    add_chunk((narrow + n_narrow - d - 1) % n_narrow, False)

    def activate(t, carry):
        columns = lane_block(t, tile)
        if chunked:
            value = hidden[:, columns]
            back_value = back[:, columns]
        else:
            value = jnp.dot(pooled[...], w1[:, columns], preferred_element_type=jnp.float32)
            back_value = lax.dot_general(
                cot[...], w2[columns, :], NT, preferred_element_type=jnp.float32
            )
        value = value + bias_ref[:, columns]
        sig = jax.nn.sigmoid(value)
        slopes = sig * (1.0 + value * (1.0 - sig))
        deltas[:, columns] = (back_value * slopes).astype(jnp.bfloat16)
        return carry

    lax.fori_loop(0, inner // tile, activate, 0)

    for d in range(rest):
        source = (narrow + n_narrow - d - 1) % n_narrow
        view = looks.at[source]
        remote(view, view, send_sem, crecv_sem.at[d], {"narrow": source}).wait_recv()

    groups = tables // 2
    for t in range(groups):
        wrows = w1[2 * t * emb:2 * (t + 1) * emb, :]
        grad_in = lax.dot_general(
            deltas[...], wrows, NT, preferred_element_type=jnp.float32
        ).astype(jnp.bfloat16)
        for i in range(2):
            k = 2 * t + i
            lookups = looks[:, k].reshape(n_narrow * slots, bags)
            value = jnp.dot(
                lookups, grad_in[:, i * emb:(i + 1) * emb], preferred_element_type=jnp.float32
            )
            for owner in range(n_narrow):
                rows = value[owner * slots:(owner + 1) * slots]
                gfull[owner, k] = rows
                gsend[owner, k] = rows.astype(jnp.bfloat16)
        block = pl.ds(2 * t, 2)
        for d in range(rest):
            owner = (narrow + d + 1) % n_narrow
            launch(remote(
                gsend.at[owner, block], grecv.at[narrow, block],
                send_sem, grecv_sem.at[d, t], {"narrow": owner},
            ))
    for t in range(groups):
        block = pl.ds(2 * t, 2)
        total = gfull[narrow, block]
        for d in range(rest):
            source = (narrow + n_narrow - d - 1) % n_narrow
            view = grecv.at[source, block]
            remote(view, view, send_sem, grecv_sem.at[d, t], {"narrow": source}).wait_recv()
            total = total + grecv[source, block].astype(jnp.float32)
        grads = total * scale
        norms = jnp.sqrt(jnp.sum(grads * grads, axis=-1, keepdims=True))
        sums[wide, block] = (grads * (limit / jnp.maximum(norms, limit))).astype(jnp.bfloat16)
        for e in range(n_wide - 1):
            launch(remote(
                sums.at[wide, block], sums.at[wide, block],
                send_sem, arecv_sem.at[t, e], {"wide": (wide + e + 1) % n_wide},
            ))
    for t in range(groups):
        block = pl.ds(2 * t, 2)
        for e in range(n_wide - 1):
            source = (wide + n_wide - e - 1) % n_wide
            view = sums.at[source, block]
            remote(view, view, send_sem, arecv_sem.at[t, e], {"wide": source}).wait_recv()
        summed = sums[0, block].astype(jnp.float32)
        for q in range(1, n_wide):
            summed = summed + sums[q, block].astype(jnp.float32)
        for i in range(2):
            k = 2 * t + i
            hot = lax.broadcasted_iota(jnp.int32, (out_ref.shape[1], slots), 0) == ids_ref[k:k + 1, :]
            out_ref[k] = jnp.dot(
                hot.astype(jnp.float32), summed[i], precision=lax.Precision.HIGHEST,
                preferred_element_type=jnp.float32,
            )
    for copy in sent:
        copy.wait_send()


def shards(n_wide, n_narrow, pooled, cotangent, w_first, b_first, w_second, counts, row_ids, table, accum):
    tables, slots, group_bags = counts.shape
    emb = table.shape[2]
    bags, emb_all = pooled.shape
    shard, inner = w_first.shape
    top = w_second.shape[1]
    pieces = pieces_of(shard, n_wide)
    rest = n_narrow - 1
    groups = tables // 2
    scale = 1.0 / math.sqrt(group_bags)
    limit = clip_factor * math.sqrt(emb)
    hbm = pl.BlockSpec(memory_space=pl.ANY)
    vmem = pl.BlockSpec(memory_space=pltpu.VMEM)
    dma = pltpu.SemaphoreType.DMA
    summed = pl.pallas_call(
        functools.partial(tower_kernel, n_wide, n_narrow, pieces, scale, limit),
        out_shape=jax.ShapeDtypeStruct(table.shape, jnp.float32),
        in_specs=[hbm, hbm, hbm, hbm, vmem, hbm, vmem],
        out_specs=vmem,
        scratch_shapes=[
            pltpu.VMEM((bags, emb_all), jnp.bfloat16),
            pltpu.VMEM((bags, top), jnp.bfloat16),
            pltpu.VMEM((emb_all, inner), jnp.bfloat16),
            pltpu.VMEM((inner, top), jnp.bfloat16),
            pltpu.VMEM((n_narrow, tables, slots, bags), jnp.bfloat16),
            pltpu.VMEM((bags, inner), jnp.float32),
            pltpu.VMEM((bags, inner), jnp.float32),
            pltpu.VMEM((bags, inner), jnp.bfloat16),
            pltpu.VMEM((n_narrow, tables, slots, emb), jnp.float32),
            pltpu.VMEM((n_narrow, tables, slots, emb), jnp.bfloat16),
            pltpu.VMEM((n_narrow, tables, slots, emb), jnp.bfloat16),
            pltpu.VMEM((n_wide, tables, slots, emb), jnp.bfloat16),
            dma((5,)),
            dma,
            dma((3, rest, pieces)),
            dma((rest,)),
            dma((rest, groups)),
            dma((groups, n_wide - 1)),
        ],
        compiler_params=pltpu.CompilerParams(
            collective_id=0, has_side_effects=True, vmem_limit_bytes=56 * 1024 * 1024
        ),
        name="tower",
    )(pooled, cotangent, w_first, w_second, b_first.reshape(1, inner), counts, row_ids)
    new_accum = accum + summed * summed
    return table - learn_rate * summed / (jnp.sqrt(new_accum) + epsilon), new_accum


def solution(mesh):
    in_specs = (
        P(("wide", "narrow"), None),
        P(("wide", "narrow"), None),
        P("narrow", None),
        P(),
        P("narrow", None),
        P(None, "narrow", "wide"),
        P(None, "narrow"),
        P(None, "narrow", None),
        P(None, "narrow", None),
    )
    out_specs = (P(None, "narrow", None), P(None, "narrow", None))
    step = functools.partial(shards, mesh.shape["wide"], mesh.shape["narrow"])
    return jax.shard_map(step, mesh=mesh, in_specs=in_specs, out_specs=out_specs, check_vma=False)
```

```python
import functools
import math

import jax
import jax.numpy as jnp
from jax import lax
from jax.experimental import pallas as pl
from jax.experimental.pallas import tpu as pltpu
from jax.sharding import PartitionSpec as P

MESH = pl.DeviceIdType.MESH
clip_factor = 0.5
learn_rate = 0.05
epsilon = 1e-08
NT = (((1,), (1,)), ((), ()))
ROUTES = ("xy", "yx", "hw")
DEFER = 8
LAG_SIDE = 6
LAG_DIAG = 10
VMEM_KIB = 32 * 1024


def flip(index, mask):
    bit = 1
    while bit <= mask:
        if mask & bit:
            index = index + bit * (1 - 2 * ((index // bit) % 2))
        bit *= 2
    return index


def pieces_of(shard_rows, n_wide):
    pieces = 1
    while pieces < 8 and n_wide % (2 * pieces) == 0 and shard_rows % (32 * pieces) == 0:
        pieces *= 2
    return pieces


def arrivals(n, n_narrow, count):
    items = []
    for s in range(n_narrow):
        if s != n:
            for v in range(count):
                items.append(((abs(s - n) - 1) * count + v, s > n, s, v))
    return [(s, v) for _, _, s, v in sorted(items)]


def tower_kernel(
    n_wide, n_narrow, pieces, scale, limit,
    pooled_hbm, cot_hbm, w1_hbm, w2_hbm, bias_hbm, counts_hbm, ids_hbm, out_ref,
    pooled, cot, weights, bias, ids, looks, hidden, back, deltas, grad_in, gfull, gsend, grecv, sums,
    local_sem, send_sem, z_sem, x_sem, y_sem, d_sem, c_sem, look_sem, grad_sem, sum_sem,
):
    wide = lax.axis_index("wide")
    narrow = lax.axis_index("narrow")
    shard, inner = w1_hbm.shape
    top = w2_hbm.shape[1]
    units = inner // top + 1
    piece_rows = shard // pieces
    bags = pooled.shape[0]
    emb = gfull.shape[3]
    tables, slots = looks.shape[1], looks.shape[2]
    rest = n_narrow - 1
    part = wide % pieces
    base = wide - part
    has_core, has_x, has_y = pieces >= 2, pieces >= 4, pieces >= 8
    routes = [ROUTES[u % len(ROUTES)] for u in range(units)] if has_y else ["none"] * units
    chained = [u for u in range(units) if routes[u] == "z"]
    per_source = units + len(chained)

    def lane_block(index, size):
        return pl.ds(pl.multiple_of(index * size, size), size)

    def local(step, src, dst):
        return pltpu.make_async_copy(src, dst, local_sem.at[step])

    own_rows = lane_block(narrow, shard)
    own_w = [
        local(0, w1_hbm, weights.at[own_rows, pl.ds(0, inner)]),
        local(1, w2_hbm, weights.at[own_rows, pl.ds(inner, top)]),
    ]
    own_x = [local(2, pooled_hbm, pooled), local(3, cot_hbm, cot)]
    own_rest = [
        local(4, counts_hbm.at[:, :, lane_block(narrow, bags)], looks.at[narrow]),
        local(5, bias_hbm, bias),
        local(6, ids_hbm, ids),
    ]
    for copy in own_w + own_x + own_rest:
        copy.start()

    barrier = pltpu.get_barrier_semaphore()

    def greet(device):
        pl.semaphore_signal(barrier, inc=1, device_id=device, device_id_type=MESH)

    @pl.when(narrow > 0)
    def _():
        greet({"narrow": narrow - 1})

    @pl.when(narrow < n_narrow - 1)
    def _():
        greet({"narrow": narrow + 1})

    if pieces == n_wide:
        beside = [base + flip(part, m) for m in (1, 2, 4) if m < pieces]
    else:
        beside = [(wide + d) % n_wide for d in range(1, n_wide)]
    for device in beside:
        greet({"wide": device})
    ends = jnp.where(narrow > 0, 1, 0) + jnp.where(narrow < n_narrow - 1, 1, 0)
    pl.semaphore_wait(barrier, ends + len(beside))

    def remote(src, dst, recv, device):
        return pltpu.make_async_remote_copy(
            src_ref=src, dst_ref=dst, send_sem=send_sem, recv_sem=recv,
            device_id=device, device_id_type=MESH,
        )

    sent = []

    def launch(copy, cond=None):
        if cond is None:
            copy.start()
        else:
            @pl.when(cond)
            def _():
                copy.start()
        sent.append((copy, cond))

    def pick(values):
        if all(v == values[0] for v in values):
            return values[0]
        total = 0
        for n, v in enumerate(values):
            total = total + jnp.where(narrow == n, v, 0)
        return total

    def slot_of(s, n):
        return (s - n + n_narrow) % n_narrow - 1

    def view(s, q, u):
        rows = pl.ds(pl.multiple_of(s * shard + q * piece_rows, piece_rows), piece_rows)
        return weights.at[rows, lane_block(u, top)]

    def any_of(u, chosen):
        hit = u == chosen[0]
        for c in chosen[1:]:
            hit = jnp.logical_or(hit, u == c)
        return hit

    def on_route(s, u, route):
        if route == "hw":
            return False
        return (u + jnp.where(u == units - 1, s, 0)) % 2 == (0 if route == "xy" else 1)

    for copy in own_w:
        copy.wait()
    for v in range(per_source):
        u = v if v < units else chained[v - units]
        q = part if v < units else flip(part, 6)
        w = view(narrow, q, u)
        for ahead, cond in ((narrow + 1, narrow < n_narrow - 1), (narrow - 1, narrow > 0)):
            launch(remote(w, w, z_sem.at[slot_of(narrow, ahead), v], {"narrow": ahead}), cond)

    order = [arrivals(n, n_narrow, per_source) for n in range(n_narrow)]
    side = [[(s, v) for s, v in order[n] if v < units] for n in range(n_narrow)]
    diag = [[(s, v) for s, v in side[n] if routes[v] != "z"] for n in range(n_narrow)]
    n_z = len(order[0])
    side_at = [order[0].index(item) + LAG_SIDE for item in side[0]]
    diag_at = [order[0].index(item) + LAG_DIAG for item in diag[0]]
    if not has_x:
        side_at = []
    if not has_y:
        diag_at = []

    def to_core(w, slot):
        if has_core:
            launch(remote(w, w, c_sem.at[slot], {"wide": base + flip(part, 1)}))

    def await_view(w, sem):
        remote(w, w, sem, {"wide": base + flip(part, 1)} if has_core else {"narrow": narrow}).wait_recv()

    def z_event(t):
        s, v = pick([o[t][0] for o in order]), pick([o[t][1] for o in order])
        slot = slot_of(s, narrow)
        u, q, mine = v, part, None
        if chained:
            mine = v < units
            extra = 0
            for i, c in enumerate(chained):
                extra = extra + jnp.where(v == units + i, c, 0)
            u = jnp.where(mine, v, extra)
            q = jnp.where(mine, part, flip(part, 6))
        w = view(s, q, u)
        await_view(w, z_sem.at[slot, v])
        ahead = jnp.where(s < narrow, narrow + 1, narrow - 1)
        inside = jnp.logical_and(ahead >= 0, ahead < n_narrow)
        launch(remote(w, w, z_sem.at[slot_of(s, ahead), v], {"narrow": ahead}), inside)
        if has_x:
            launch(remote(w, w, x_sem.at[slot, u], {"wide": base + flip(part, 2)}), mine)
        if has_y:
            launch(remote(w, w, y_sem.at[slot, u], {"wide": base + flip(part, 4)}), mine)
            direct = on_route(s, u, "hw")
            if direct is not False:
                if mine is not None:
                    direct = jnp.logical_and(direct, mine)
                launch(remote(w, w, d_sem.at[slot, u], {"wide": base + flip(part, 6)}), direct)
        to_core(w, slot)

    def side_event(j):
        s, u = pick([o[j][0] for o in side]), pick([o[j][1] for o in side])
        slot = slot_of(s, narrow)
        for name, mask, sem, there, route in (
            ("x", 2, x_sem, 4, "xy"), ("y", 4, y_sem, 2, "yx"),
        ):
            if mask < pieces:
                w = view(s, flip(part, mask), u)
                await_view(w, sem.at[slot, u])
                onward = on_route(s, u, route)
                if onward is not False:
                    launch(remote(w, w, d_sem.at[slot, u], {"wide": base + flip(part, there)}), onward)
                to_core(w, slot)

    def diag_event(j):
        s, u = pick([o[j][0] for o in diag]), pick([o[j][1] for o in diag])
        slot = slot_of(s, narrow)
        w = view(s, flip(part, 6), u)
        await_view(w, d_sem.at[slot, u])
        to_core(w, slot)

    def add_chunk(source, fresh):
        rows = lane_block(source, shard)
        value = jnp.dot(
            pooled[:, rows], weights[rows, pl.ds(0, inner)], preferred_element_type=jnp.float32
        )
        if fresh:
            hidden[...] = value
        else:
            hidden[...] = hidden[...] + value
        back[:, rows] = lax.dot_general(
            cot[...], weights[rows, pl.ds(inner, top)], NT, preferred_element_type=jnp.float32
        )

    groups = tables // 2
    dests = []
    for n in range(n_narrow):
        plan = []
        for owner in range(n_narrow):
            if owner == n:
                continue
            seen = -1 if abs(owner - n) == 1 else order[n].index((owner, 0))
            relays = [t for t, (s, v) in enumerate(order[n]) if (s < n) == (owner > n)]
            plan.append((DEFER, abs(owner - n), owner))
        dests.append(sorted(plan))

    def send_looks(t):
        most = max(len([p for p in dests[n] if p[0] == t]) for n in range(n_narrow))
        if not most:
            return
        chosen = []
        for i in range(most):
            rows = [[p[2] for p in dests[n] if p[0] == t] for n in range(n_narrow)]
            owner = pick([r[i] if i < len(r) else (n + 1) % n_narrow for n, r in enumerate(rows)])
            valid = pick([1 if i < len(r) else 0 for r in rows])
            chosen.append((owner, valid))
        for g in range(groups):
            block = pl.ds(2 * g, 2)
            for owner, valid in chosen:
                launch(
                    remote(
                        counts_hbm.at[block, :, lane_block(owner, bags)], looks.at[narrow, block],
                        look_sem.at[g], {"narrow": owner},
                    ),
                    None if isinstance(valid, int) else valid == 1,
                )

    send_looks(-1)
    chunked = shard % 128 == 0
    for copy in own_x:
        copy.wait()
    if chunked:
        add_chunk(narrow, True)

    ranks = []
    for n in range(n_narrow):
        done = {}
        for t, (s, v) in enumerate(order[n]):
            done[s] = max(done.get(s, 0), t)
        for at, items in ((side_at, side[n]), (diag_at, diag[n])):
            for t, (s, v) in zip(at, items):
                done[s] = max(done[s], t)
        ranks.append(sorted((t, s) for s, t in done.items()))
    steps = max([n_z] + [t + 1 for t in side_at + diag_at])
    ready = [steps - 1] * rest
    for t in range(steps):
        if t < n_z:
            z_event(t)
        send_looks(t)
        if t in side_at:
            side_event(side_at.index(t))
        if t in diag_at:
            diag_event(diag_at.index(t))
        for i in range(rest):
            if ready[i] == t:
                s = pick([r[i][1] for r in ranks])
                if has_core:
                    w = weights.at[pl.ds(0, shard // 2), :]
                    await_view(w, c_sem.at[slot_of(s, narrow)])
                if chunked:
                    add_chunk(s, False)

    for copy in own_rest:
        copy.wait()
    if not chunked:
        hidden[...] = jnp.dot(
            pooled[...], weights[:, pl.ds(0, inner)], preferred_element_type=jnp.float32
        )
        back[...] = lax.dot_general(
            cot[...], weights[:, pl.ds(inner, top)], NT, preferred_element_type=jnp.float32
        )
    tile = min(256, inner)

    def activate(t, carry):
        columns = lane_block(t, tile)
        value = hidden[:, columns] + bias[:, columns]
        sig = jax.nn.sigmoid(value)
        slopes = sig * (1.0 + value * (1.0 - sig))
        deltas[:, columns] = (back[:, columns] * slopes).astype(jnp.bfloat16)
        return carry

    lax.fori_loop(0, inner // tile, activate, 0)

    far = [[s for _, s in sorted((-abs(s - n), s) for s in range(n_narrow) if s != n)] for n in range(n_narrow)]
    grad_in[...] = lax.dot_general(
        deltas[...], weights[:, pl.ds(0, inner)], NT, preferred_element_type=jnp.float32
    ).astype(jnp.bfloat16)
    for g in range(groups):
        await_view(looks.at[pl.ds(0, rest), pl.ds(2 * g, 2)], look_sem.at[g])
    for g in range(groups):
        lookups = looks[:, 2 * g:2 * (g + 1)].reshape(n_narrow * 2 * slots, bags)
        value = jnp.dot(
            lookups, grad_in[:, 2 * g * emb:2 * (g + 1) * emb], preferred_element_type=jnp.float32
        )
        value = value.reshape(n_narrow, 2, slots, 2 * emb)
        for i in range(2):
            rows = value[:, i, :, i * emb:(i + 1) * emb]
            gfull[:, 2 * g + i] = rows
            gsend[:, 2 * g + i] = rows.astype(jnp.bfloat16)
    for g in range(groups):
        block = pl.ds(2 * g, 2)
        for i in range(rest):
            owner = pick([f[i] for f in far])
            launch(remote(
                gsend.at[owner, block], grecv.at[slot_of(narrow, owner), block],
                grad_sem.at[g], {"narrow": owner},
            ))
    for g in range(groups):
        block = pl.ds(2 * g, 2)
        await_view(grecv.at[:, block], grad_sem.at[g])
        total = gfull[narrow, block]
        for d in range(rest):
            total = total + grecv[d, block].astype(jnp.float32)
        grads = total * scale
        norms = jnp.sqrt(jnp.sum(grads * grads, axis=-1, keepdims=True))
        sums[wide, block] = (grads * (limit / jnp.maximum(norms, limit))).astype(jnp.bfloat16)
        for e in range(n_wide - 1, 0, -1):
            peer = base + flip(part, e) if pieces == n_wide else (wide + e) % n_wide
            launch(remote(
                sums.at[wide, block], sums.at[wide, block], sum_sem.at[g], {"wide": peer},
            ))
    for g in range(groups):
        block = pl.ds(2 * g, 2)
        await_view(sums.at[pl.ds(0, n_wide - 1), block], sum_sem.at[g])
        summed = sums[0, block].astype(jnp.float32)
        for q in range(1, n_wide):
            summed = summed + sums[q, block].astype(jnp.float32)
        for i in range(2):
            k = 2 * g + i
            hot = lax.broadcasted_iota(jnp.int32, (out_ref.shape[1], slots), 0) == ids[k:k + 1, :]
            out_ref[k] = jnp.dot(
                hot.astype(jnp.float32), summed[i], precision=lax.Precision.HIGHEST,
                preferred_element_type=jnp.float32,
            )
    for copy, cond in sent:
        if cond is None:
            copy.wait_send()
        else:
            @pl.when(cond)
            def _():
                copy.wait_send()


def shards(n_wide, n_narrow, pooled, cotangent, w_first, b_first, w_second, counts, row_ids, table, accum):
    tables, slots, group_bags = counts.shape
    emb = table.shape[2]
    bags, emb_all = pooled.shape
    shard, inner = w_first.shape
    top = w_second.shape[1]
    units = inner // top + 1
    pieces = pieces_of(shard, n_wide)
    rest = n_narrow - 1
    groups = tables // 2
    scale = 1.0 / math.sqrt(group_bags)
    limit = clip_factor * math.sqrt(emb)
    hbm = pl.BlockSpec(memory_space=pl.ANY)
    vmem = pl.BlockSpec(memory_space=pltpu.VMEM)
    dma = pltpu.SemaphoreType.DMA
    summed = pl.pallas_call(
        functools.partial(tower_kernel, n_wide, n_narrow, pieces, scale, limit),
        out_shape=jax.ShapeDtypeStruct(table.shape, jnp.float32),
        in_specs=[hbm] * 7,
        out_specs=vmem,
        scratch_shapes=[
            pltpu.VMEM((bags, emb_all), jnp.bfloat16),
            pltpu.VMEM((bags, top), jnp.bfloat16),
            pltpu.VMEM((emb_all, inner + top), jnp.bfloat16),
            pltpu.VMEM((1, inner), jnp.float32),
            pltpu.VMEM(row_ids.shape, jnp.int32),
            pltpu.VMEM((n_narrow, tables, slots, bags), jnp.bfloat16),
            pltpu.VMEM((bags, inner), jnp.float32),
            pltpu.VMEM((bags, inner), jnp.float32),
            pltpu.VMEM((bags, inner), jnp.bfloat16),
            pltpu.VMEM((bags, emb_all), jnp.bfloat16),
            pltpu.VMEM((n_narrow, tables, slots, emb), jnp.float32),
            pltpu.VMEM((n_narrow, tables, slots, emb), jnp.bfloat16),
            pltpu.VMEM((rest, tables, slots, emb), jnp.bfloat16),
            pltpu.VMEM((n_wide, tables, slots, emb), jnp.bfloat16),
            dma((7,)),
            dma,
            dma((rest, units + len([r for r in ROUTES if r == "z"]))),
            dma((rest, units)),
            dma((rest, units)),
            dma((rest, units)),
            dma((rest,)),
            dma((groups,)),
            dma((groups,)),
            dma((groups,)),
        ],
        compiler_params=pltpu.CompilerParams(
            collective_id=0, has_side_effects=True, vmem_limit_bytes=VMEM_KIB * 1024
        ),
        name="tower",
    )(*[
        pltpu.with_memory_space_constraint(x, pltpu.HBM)
        for x in (pooled, cotangent, w_first, w_second, b_first.reshape(1, inner), counts, row_ids)
    ])
    new_accum = accum + summed * summed
    return table - learn_rate * summed / (jnp.sqrt(new_accum) + epsilon), new_accum


def solution(mesh):
    in_specs = (
        P(("wide", "narrow"), None),
        P(("wide", "narrow"), None),
        P("narrow", None),
        P(),
        P("narrow", None),
        P(None, "narrow", "wide"),
        P(None, "narrow"),
        P(None, "narrow", None),
        P(None, "narrow", None),
    )
    out_specs = (P(None, "narrow", None), P(None, "narrow", None))
    step = functools.partial(shards, mesh.shape["wide"], mesh.shape["narrow"])
    return jax.shard_map(step, mesh=mesh, in_specs=in_specs, out_specs=out_specs, check_vma=False)
```

```python
import functools
import math

import jax
import jax.numpy as jnp
from jax import lax
from jax.experimental import pallas as pl
from jax.experimental.pallas import tpu as pltpu
from jax.sharding import PartitionSpec as P

MESH = pl.DeviceIdType.MESH
clip_factor = 0.5
learn_rate = 0.05
epsilon = 1e-08
NT = (((1,), (1,)), ((), ()))
HOP_Z = 3.0
STEP_Z = 0.35
PACE = 0.0
HOP_S = 3.4
HOP_D = 3.4
HOP_C = 1.4
HOP_W = 4.0
STRAIGHT = 1
ACT_TILE = 512
Z_UNITS = ()
HALVES = 2
VMEM_KIB = 32 * 1024


def flip(index, mask):
    bit = 1
    while bit <= mask:
        if mask & bit:
            index = index + bit * (1 - 2 * ((index // bit) % 2))
        bit *= 2
    return index


def pieces_of(shard_rows, n_wide):
    pieces = 1
    while pieces < 8 and n_wide % (2 * pieces) == 0 and shard_rows % (32 * pieces) == 0:
        pieces *= 2
    return pieces


def arrivals(n, n_narrow, count):
    items = []
    for s in range(n_narrow):
        if s != n:
            for v in range(count):
                items.append(((abs(s - n) - 1) * count + v, s > n, s, v))
    return [(s, v) for _, _, s, v in sorted(items)]


def tower_kernel(
    n_wide, n_narrow, pieces, scale, limit,
    pooled_hbm, cot_hbm, w1_hbm, w2_hbm, bias_hbm, counts_hbm, ids_hbm, out_ref,
    pooled, cot, weights, bias, ids, looks, hidden, back, deltas, grad_in, gfull, gsend, grecv, sums,
    local_sem, send_sem, z_sem, x_sem, y_sem, d_sem, c_sem, look_sem, grad_sem, sum_sem,
):
    wide = lax.axis_index("wide")
    narrow = lax.axis_index("narrow")
    shard, inner = w1_hbm.shape
    top = w2_hbm.shape[1]
    units = inner // top + 1
    piece_rows = shard // pieces
    bags = pooled.shape[0]
    emb = gfull.shape[3]
    tables, slots = looks.shape[1], looks.shape[2]
    rest = n_narrow - 1
    part = wide % pieces
    base = wide - part
    has_core, has_x, has_y = pieces >= 2, pieces >= 4, pieces >= 8
    def lane_block(index, size):
        return pl.ds(pl.multiple_of(index * size, size), size)

    def local(step, src, dst):
        return pltpu.make_async_copy(src, dst, local_sem.at[step])

    own_rows = lane_block(narrow, shard)
    own_w = [
        local(0, w1_hbm, weights.at[own_rows, pl.ds(0, inner)]),
        local(1, w2_hbm, weights.at[own_rows, pl.ds(inner, top)]),
    ]
    own_x = [local(2, pooled_hbm, pooled), local(3, cot_hbm, cot)]
    own_rest = [
        local(4, counts_hbm.at[:, :, lane_block(narrow, bags)], looks.at[narrow]),
        local(5, bias_hbm, bias),
        local(6, ids_hbm, ids),
    ]
    for copy in own_w + own_x + own_rest:
        copy.start()

    barrier = pltpu.get_barrier_semaphore()

    def greet(device):
        pl.semaphore_signal(barrier, inc=1, device_id=device, device_id_type=MESH)

    @pl.when(narrow > 0)
    def _():
        greet({"narrow": narrow - 1})

    @pl.when(narrow < n_narrow - 1)
    def _():
        greet({"narrow": narrow + 1})

    if pieces == n_wide:
        beside = [base + flip(part, m) for m in (1, 2, 4) if m < pieces]
    else:
        beside = [(wide + d) % n_wide for d in range(1, n_wide)]
    for device in beside:
        greet({"wide": device})
    ends = jnp.where(narrow > 0, 1, 0) + jnp.where(narrow < n_narrow - 1, 1, 0)
    pl.semaphore_wait(barrier, ends + len(beside))

    def remote(src, dst, recv, device):
        return pltpu.make_async_remote_copy(
            src_ref=src, dst_ref=dst, send_sem=send_sem, recv_sem=recv,
            device_id=device, device_id_type=MESH,
        )

    sent = []

    def launch(copy, cond=None):
        if cond is None:
            copy.start()
        else:
            @pl.when(cond)
            def _():
                copy.start()
        sent.append((copy, cond))

    def pick(values):
        if all(v == values[0] for v in values):
            return values[0]
        total = 0
        for n, v in enumerate(values):
            total = total + jnp.where(narrow == n, v, 0)
        return total

    def slot_of(s, n):
        return (s - n + n_narrow) % n_narrow - 1

    def view(s, q, u):
        rows = pl.ds(pl.multiple_of(s * shard + q * piece_rows, piece_rows), piece_rows)
        return weights.at[rows, lane_block(u, top)]

    crosses = [u for u in range(units) if has_y and n_narrow <= 4 and u in Z_UNITS]

    def piece_of(s, v):
        if crosses and v >= units:
            return view(s, flip(part, 6), crosses[v - units])
        return view(s, part, v)

    for copy in own_w:
        copy.wait()
    for v in range(units + len(crosses)):
        w = piece_of(narrow, v)
        for ahead, cond in ((narrow + 1, narrow < n_narrow - 1), (narrow - 1, narrow > 0)):
            launch(remote(w, w, z_sem.at[slot_of(narrow, ahead), v], {"narrow": ahead}), cond)

    order = [arrivals(n, n_narrow, units + len(crosses)) for n in range(n_narrow)]
    groups = tables // 2
    ranks = [sorted((s for s in range(n_narrow) if s != n), key=lambda s: (abs(s - n), s > n)) for n in range(n_narrow)]

    def await_view(w, sem):
        remote(w, w, sem, {"narrow": (narrow + 1) % n_narrow}).wait_recv()

    class Role:
        def __init__(self, members):
            self.members = members
            self.started = 0
            self.looks = 0

        def item(self, j):
            pairs = [order[n][j] if n in self.members else (-1, -1) for n in range(n_narrow)]
            fill = order[self.members[0]][j]
            pairs = [fill if p[0] < 0 else p for p in pairs]
            s, u = pick([p[0] for p in pairs]), pick([p[1] for p in pairs])
            assert not crosses or isinstance(u, int)
            return s, u, slot_of(s, narrow)

        def send(self, w, sem, device):
            remote(w, w, sem, device).start()
            self.started += 1

        def straight(self, j):
            return has_y and all(order[n][j][0] in ranks[n][rest - STRAIGHT:] for n in self.members) and (
                not crosses or order[self.members[0]][j][1] not in crosses
            )

        def to_core(self, w, slot):
            if has_core:
                self.send(w, c_sem.at[slot], {"wide": base + flip(part, 1)})

        def chain(self, j):
            s, u, slot = self.item(j)
            w = piece_of(s, u)
            await_view(w, z_sem.at[slot, u])
            if 0 not in self.members:
                ahead = jnp.where(s < narrow, narrow + 1, narrow - 1)
                self.send(w, z_sem.at[slot_of(s, ahead), u], {"narrow": ahead})
            if crosses and u >= units:
                self.to_core(w, slot)

        def plane(self, j):
            s, u, slot = self.item(j)
            w = view(s, part, u)
            if has_x:
                self.send(w, x_sem.at[slot, u], {"wide": base + flip(part, 2)})
            if has_y:
                self.send(w, y_sem.at[slot, u], {"wide": base + flip(part, 4)})
            if self.straight(j):
                self.send(w, d_sem.at[slot, u], {"wide": base + flip(part, 6)})
            self.to_core(w, slot)

        def side(self, j):
            s, u, slot = self.item(j)
            odd = (s if crosses else u + jnp.where(u == units - 1, s, 0)) % 2
            for name, mask, sem, there, turn in (("x", 2, x_sem, 4, 0), ("y", 4, y_sem, 2, 1)):
                if mask < pieces:
                    w = view(s, flip(part, mask), u)
                    await_view(w, sem.at[slot, u])
                    if has_y and not (crosses and u in crosses) and not self.straight(j):
                        onward = remote(w, w, d_sem.at[slot, u], {"wide": base + flip(part, there)})

                        @pl.when(odd == turn)
                        def _():
                            onward.start()
                    self.to_core(w, slot)
            if has_y and not (crosses and u in crosses) and not self.straight(j):
                self.started += 1

        def corner(self, j):
            s, u, slot = self.item(j)
            w = view(s, flip(part, 6), u)
            await_view(w, d_sem.at[slot, u])
            self.to_core(w, slot)

        def gathered(self, i):
            s = pick([ranks[n][i] if n in self.members else ranks[self.members[0]][i] for n in range(n_narrow)])
            if has_core:
                await_view(weights.at[pl.ds(0, shard // 2), :], c_sem.at[slot_of(s, narrow)])
            if chunked and i < rest - 1:
                add_chunk(s, False)

        def lookups(self, d):
            for g in range(groups):
                block = pl.ds(2 * g, 2)
                for side in (narrow - d, narrow + d):
                    valid = jnp.logical_and(side >= 0, side < n_narrow)
                    copy = remote(
                        counts_hbm.at[block, :, lane_block(jnp.where(valid, side, 0), bags)],
                        looks.at[narrow, block], look_sem.at[g], {"narrow": jnp.where(valid, side, (narrow + 1) % n_narrow)},
                    )

                    @pl.when(valid)
                    def _():
                        copy.start()

        def settle(self):
            most = weights.shape[0] // piece_rows
            count = self.started
            while count > 0:
                k = min(count, most)
                w = weights.at[pl.ds(0, k * piece_rows), pl.ds(0, top)]
                remote(w, w, c_sem.at[0], {"narrow": (narrow + 1) % n_narrow}).wait_send()
                count -= k

    def add_chunk(source, fresh):
        rows = lane_block(source, shard)
        value = jnp.dot(
            pooled[:, rows], weights[rows, pl.ds(0, inner)], preferred_element_type=jnp.float32
        )
        if fresh:
            hidden[...] = value
        else:
            hidden[...] = hidden[...] + value
        back[:, rows] = lax.dot_general(
            cot[...], weights[rows, pl.ds(inner, top)], NT, preferred_element_type=jnp.float32
        )

    chunked = shard % 128 == 0
    for copy in own_x:
        copy.wait()
    if chunked:
        add_chunk(narrow, True)

    roles = [Role([n for n in (0, n_narrow - 1)])]
    if n_narrow > 2:
        roles.append(Role(list(range(1, n_narrow - 1))))
    for r, role in enumerate(roles):
        n = role.members[0]
        plan = []
        at = {}
        placed = 0
        for j, (s, u) in enumerate(order[n]):
            z = HOP_Z * abs(s - n) + STEP_Z * u
            plan.append((z, 0, role.chain, j))
            last = z
            if u < units:
                p = z if r == 0 else max(z, HOP_Z + PACE * placed)
                if role.straight(j):
                    p = max(p, HOP_Z + HOP_S + 0.01)
                placed += 1
                plan.append((p, 1, role.plane, j))
                last = p
                if has_x:
                    last = p + HOP_S
                    plan.append((last, 2, role.side, j))
                if has_y and u not in crosses:
                    last = p + (HOP_W if role.straight(j) else HOP_S + HOP_D)
                    plan.append((last, 3, role.corner, j))
            at[s] = max(last, at.get(s, 0.0))
        done = max(t for t, _, kind, _ in plan if kind == role.chain)
        for d in range(1, n_narrow):
            early = r == 0 and d == 1
            plan.append((0.0 if early else done, 1.5, role.lookups, d))
        for i in range(rest):
            s = ranks[n][i]
            plan.append((at[s] + HOP_C, 4, role.gathered, i))
        plan.sort(key=lambda e: e[:2])
        kinds = [(e[2], e[3]) for e in plan]
        for j in range(len(order[n])):
            if order[n][j][1] < units and role.straight(j):
                assert kinds.index((role.side, 0)) < kinds.index((role.plane, j))

        @pl.when(jnp.logical_or(narrow == 0, narrow == n_narrow - 1) if r == 0 else jnp.logical_and(narrow > 0, narrow < n_narrow - 1))
        def _():
            for _, _, event, j in plan:
                event(j)

    for copy in own_rest:
        copy.wait()
    tile = min(ACT_TILE, inner)
    if chunked:
        last = lane_block(pick([r[rest - 1] for r in ranks]), shard)
        back[:, last] = lax.dot_general(
            cot[...], weights[last, pl.ds(inner, top)], NT, preferred_element_type=jnp.float32
        )
    for t in range(inner // tile):
        columns = pl.ds(t * tile, tile)
        if chunked:
            value = hidden[:, columns] + jnp.dot(
                pooled[:, last], weights[last, columns], preferred_element_type=jnp.float32
            )
            back_value = back[:, columns]
        else:
            value = jnp.dot(pooled[...], weights[:, columns], preferred_element_type=jnp.float32)
            back_value = lax.dot_general(
                cot[...], weights[columns, pl.ds(inner, top)], NT, preferred_element_type=jnp.float32
            )
        value = value + bias[:, columns]
        sig = jax.nn.sigmoid(value)
        slopes = sig * (1.0 + value * (1.0 - sig))
        deltas[:, columns] = (back_value * slopes).astype(jnp.bfloat16)
    far = [[s for _, s in sorted((-abs(s - n), s) for s in range(n_narrow) if s != n)] for n in range(n_narrow)]
    per_half = groups // HALVES if groups % HALVES == 0 else groups
    for h in range(groups // per_half):
        span = pl.ds(2 * h * per_half * emb, 2 * per_half * emb)
        grad_in[:, span] = lax.dot_general(
            deltas[...], weights[span, pl.ds(0, inner)], NT, preferred_element_type=jnp.float32
        ).astype(jnp.bfloat16)
        for g in range(h * per_half, (h + 1) * per_half):
            await_view(looks.at[pl.ds(0, rest), pl.ds(2 * g, 2)], look_sem.at[g])
        for g in range(h * per_half, (h + 1) * per_half):
            lookups = looks[:, 2 * g:2 * (g + 1)].reshape(n_narrow * 2 * slots, bags)
            value = jnp.dot(
                lookups, grad_in[:, 2 * g * emb:2 * (g + 1) * emb],
                preferred_element_type=jnp.float32,
            )
            value = value.reshape(n_narrow, 2, slots, 2 * emb)
            for i in range(2):
                rows = value[:, i, :, i * emb:(i + 1) * emb]
                gfull[:, 2 * g + i] = rows
                gsend[:, 2 * g + i] = rows.astype(jnp.bfloat16)
        for g in range(h * per_half, (h + 1) * per_half):
            block = pl.ds(2 * g, 2)
            for i in range(rest):
                owner = pick([f[i] for f in far])
                launch(remote(
                    gsend.at[owner, block], grecv.at[slot_of(narrow, owner), block],
                    grad_sem.at[g], {"narrow": owner},
                ))
    for g in range(groups):
        block = pl.ds(2 * g, 2)
        await_view(grecv.at[:, block], grad_sem.at[g])
        total = gfull[narrow, block]
        for d in range(rest):
            total = total + grecv[d, block].astype(jnp.float32)
        grads = total * scale
        norms = jnp.sqrt(jnp.sum(grads * grads, axis=-1, keepdims=True))
        sums[wide, block] = (grads * (limit / jnp.maximum(norms, limit))).astype(jnp.bfloat16)
        for e in range(n_wide - 1, 0, -1):
            peer = base + flip(part, e) if pieces == n_wide else (wide + e) % n_wide
            launch(remote(
                sums.at[wide, block], sums.at[wide, block], sum_sem.at[g], {"wide": peer},
            ))
    for g in range(groups):
        block = pl.ds(2 * g, 2)
        await_view(sums.at[pl.ds(0, n_wide - 1), block], sum_sem.at[g])
        summed = sums[0, block].astype(jnp.float32)
        for q in range(1, n_wide):
            summed = summed + sums[q, block].astype(jnp.float32)
        for i in range(2):
            k = 2 * g + i
            hot = lax.broadcasted_iota(jnp.int32, (out_ref.shape[1], slots), 0) == ids[k:k + 1, :]
            out_ref[k] = jnp.dot(
                hot.astype(jnp.float32), summed[i], precision=lax.Precision.HIGHEST,
                preferred_element_type=jnp.float32,
            )
    for g in range(groups):
        w = looks.at[pl.ds(0, rest), pl.ds(2 * g, 2)]
        remote(w, w, c_sem.at[0], {"narrow": (narrow + 1) % n_narrow}).wait_send()
    for r, role in enumerate(roles):
        @pl.when(jnp.logical_or(narrow == 0, narrow == n_narrow - 1) if r == 0 else jnp.logical_and(narrow > 0, narrow < n_narrow - 1))
        def _():
            role.settle()
    for copy, cond in sent:
        if cond is None:
            copy.wait_send()
        else:
            @pl.when(cond)
            def _():
                copy.wait_send()


def shards(n_wide, n_narrow, pooled, cotangent, w_first, b_first, w_second, counts, row_ids, table, accum):
    tables, slots, group_bags = counts.shape
    emb = table.shape[2]
    bags, emb_all = pooled.shape
    shard, inner = w_first.shape
    top = w_second.shape[1]
    units = inner // top + 1
    pieces = pieces_of(shard, n_wide)
    rest = n_narrow - 1
    groups = tables // 2
    scale = 1.0 / math.sqrt(group_bags)
    limit = clip_factor * math.sqrt(emb)
    hbm = pl.BlockSpec(memory_space=pl.ANY)
    vmem = pl.BlockSpec(memory_space=pltpu.VMEM)
    dma = pltpu.SemaphoreType.DMA
    summed = pl.pallas_call(
        functools.partial(tower_kernel, n_wide, n_narrow, pieces, scale, limit),
        out_shape=jax.ShapeDtypeStruct(table.shape, jnp.float32),
        in_specs=[hbm] * 7,
        out_specs=vmem,
        scratch_shapes=[
            pltpu.VMEM((bags, emb_all), jnp.bfloat16),
            pltpu.VMEM((bags, top), jnp.bfloat16),
            pltpu.VMEM((emb_all, inner + top), jnp.bfloat16),
            pltpu.VMEM((1, inner), jnp.float32),
            pltpu.VMEM(row_ids.shape, jnp.int32),
            pltpu.VMEM((n_narrow, tables, slots, bags), jnp.bfloat16),
            pltpu.VMEM((bags, inner), jnp.float32),
            pltpu.VMEM((bags, inner), jnp.float32),
            pltpu.VMEM((bags, inner), jnp.bfloat16),
            pltpu.VMEM((bags, emb_all), jnp.bfloat16),
            pltpu.VMEM((n_narrow, tables, slots, emb), jnp.float32),
            pltpu.VMEM((n_narrow, tables, slots, emb), jnp.bfloat16),
            pltpu.VMEM((rest, tables, slots, emb), jnp.bfloat16),
            pltpu.VMEM((n_wide, tables, slots, emb), jnp.bfloat16),
            dma((7,)),
            dma,
            dma((rest, units + len(Z_UNITS))),
            dma((rest, units)),
            dma((rest, units)),
            dma((rest, units)),
            dma((rest,)),
            dma((groups,)),
            dma((groups,)),
            dma((groups,)),
        ],
        compiler_params=pltpu.CompilerParams(
            collective_id=0, has_side_effects=True, vmem_limit_bytes=VMEM_KIB * 1024
        ),
        name="tower",
    )(*[
        pltpu.with_memory_space_constraint(x, pltpu.HBM)
        for x in (pooled, cotangent, w_first, w_second, b_first.reshape(1, inner), counts, row_ids)
    ])
    new_accum = accum + summed * summed
    return table - learn_rate * summed / (jnp.sqrt(new_accum) + epsilon), new_accum


def solution(mesh):
    in_specs = (
        P(("wide", "narrow"), None),
        P(("wide", "narrow"), None),
        P("narrow", None),
        P(),
        P("narrow", None),
        P(None, "narrow", "wide"),
        P(None, "narrow"),
        P(None, "narrow", None),
        P(None, "narrow", None),
    )
    out_specs = (P(None, "narrow", None), P(None, "narrow", None))
    step = functools.partial(shards, mesh.shape["wide"], mesh.shape["narrow"])
    return jax.shard_map(step, mesh=mesh, in_specs=in_specs, out_specs=out_specs, check_vma=False)
```

```python
import functools
import math

import jax
import jax.numpy as jnp
from jax import lax
from jax.experimental import pallas as pl
from jax.experimental.pallas import tpu as pltpu
from jax.sharding import PartitionSpec as P

MESH = pl.DeviceIdType.MESH
clip_factor = 0.5
learn_rate = 0.05
epsilon = 1e-08
NT = (((1,), (1,)), ((), ()))
HOP_Z = 3.0
STEP_Z = 0.35
PACE = 0.0
HOP_S = 3.4
HOP_D = 3.4
HOP_C = 1.4
HOP_W = 4.0
STRAIGHT = 1
END_2 = 0.0
END_3 = 0.0
MID_0 = 0.0
MID_1 = -2.6
MID_2 = 0.0
ACT_TILE = 512
Z_UNITS = (2,)
HALVES = 2
VMEM_KIB = 32 * 1024


def flip(index, mask):
    bit = 1
    while bit <= mask:
        if mask & bit:
            index = index + bit * (1 - 2 * ((index // bit) % 2))
        bit *= 2
    return index


def pieces_of(shard_rows, n_wide):
    pieces = 1
    while pieces < 8 and n_wide % (2 * pieces) == 0 and shard_rows % (32 * pieces) == 0:
        pieces *= 2
    return pieces


def arrivals(n, n_narrow, count):
    items = []
    for s in range(n_narrow):
        if s != n:
            for v in range(count):
                items.append(((abs(s - n) - 1) * count + v, s > n, s, v))
    return [(s, v) for _, _, s, v in sorted(items)]


def tower_kernel(
    n_wide, n_narrow, pieces, scale, limit,
    pooled_hbm, cot_hbm, w1_hbm, w2_hbm, bias_hbm, counts_hbm, ids_hbm, out_ref,
    pooled, cot, weights, bias, ids, looks, hidden, back, deltas, grad_in, gfull, gsend, grecv, sums,
    local_sem, send_sem, z_sem, x_sem, y_sem, d_sem, c_sem, look_sem, grad_sem, sum_sem,
):
    wide = lax.axis_index("wide")
    narrow = lax.axis_index("narrow")
    shard, inner = w1_hbm.shape
    top = w2_hbm.shape[1]
    units = inner // top + 1
    piece_rows = shard // pieces
    bags = pooled.shape[0]
    emb = gfull.shape[3]
    tables, slots = looks.shape[1], looks.shape[2]
    rest = n_narrow - 1
    part = wide % pieces
    base = wide - part
    has_core, has_x, has_y = pieces >= 2, pieces >= 4, pieces >= 8
    def lane_block(index, size):
        return pl.ds(pl.multiple_of(index * size, size), size)

    def local(step, src, dst):
        return pltpu.make_async_copy(src, dst, local_sem.at[step])

    own_rows = lane_block(narrow, shard)
    own_w = [
        local(0, w1_hbm, weights.at[own_rows, pl.ds(0, inner)]),
        local(1, w2_hbm, weights.at[own_rows, pl.ds(inner, top)]),
    ]
    own_x = [local(2, pooled_hbm, pooled), local(3, cot_hbm, cot)]
    own_rest = [
        local(4, counts_hbm.at[:, :, lane_block(narrow, bags)], looks.at[narrow]),
        local(5, bias_hbm, bias),
        local(6, ids_hbm, ids),
    ]
    for copy in own_w + own_x + own_rest:
        copy.start()

    barrier = pltpu.get_barrier_semaphore()

    def greet(device):
        pl.semaphore_signal(barrier, inc=1, device_id=device, device_id_type=MESH)

    @pl.when(narrow > 0)
    def _():
        greet({"narrow": narrow - 1})

    @pl.when(narrow < n_narrow - 1)
    def _():
        greet({"narrow": narrow + 1})

    if pieces == n_wide:
        beside = [base + flip(part, m) for m in (1, 2, 4) if m < pieces]
    else:
        beside = [(wide + d) % n_wide for d in range(1, n_wide)]
    for device in beside:
        greet({"wide": device})
    ends = jnp.where(narrow > 0, 1, 0) + jnp.where(narrow < n_narrow - 1, 1, 0)
    pl.semaphore_wait(barrier, ends + len(beside))

    def remote(src, dst, recv, device):
        return pltpu.make_async_remote_copy(
            src_ref=src, dst_ref=dst, send_sem=send_sem, recv_sem=recv,
            device_id=device, device_id_type=MESH,
        )

    sent = []

    def launch(copy, cond=None):
        if cond is None:
            copy.start()
        else:
            @pl.when(cond)
            def _():
                copy.start()
        sent.append((copy, cond))

    def pick(values):
        if all(v == values[0] for v in values):
            return values[0]
        total = 0
        for n, v in enumerate(values):
            total = total + jnp.where(narrow == n, v, 0)
        return total

    def slot_of(s, n):
        return (s - n + n_narrow) % n_narrow - 1

    def view(s, q, u):
        rows = pl.ds(pl.multiple_of(s * shard + q * piece_rows, piece_rows), piece_rows)
        return weights.at[rows, lane_block(u, top)]

    crosses = [u for u in range(units) if has_y and n_narrow <= 4 and u in Z_UNITS]

    def piece_of(s, v):
        if crosses and v >= units:
            return view(s, flip(part, 6), crosses[v - units])
        return view(s, part, v)

    for copy in own_w:
        copy.wait()
    for v in range(units + len(crosses)):
        w = piece_of(narrow, v)
        for ahead, cond in ((narrow + 1, narrow < n_narrow - 1), (narrow - 1, narrow > 0)):
            launch(remote(w, w, z_sem.at[slot_of(narrow, ahead), v], {"narrow": ahead}), cond)

    order = [arrivals(n, n_narrow, units + len(crosses)) for n in range(n_narrow)]
    groups = tables // 2
    ranks = [sorted((s for s in range(n_narrow) if s != n), key=lambda s: (abs(s - n), s > n)) for n in range(n_narrow)]

    def await_view(w, sem):
        remote(w, w, sem, {"narrow": (narrow + 1) % n_narrow}).wait_recv()

    class Role:
        def __init__(self, members):
            self.members = members
            self.started = 0
            self.looks = 0

        def item(self, j):
            pairs = [order[n][j] if n in self.members else (-1, -1) for n in range(n_narrow)]
            fill = order[self.members[0]][j]
            pairs = [fill if p[0] < 0 else p for p in pairs]
            s, u = pick([p[0] for p in pairs]), pick([p[1] for p in pairs])
            assert not crosses or isinstance(u, int)
            return s, u, slot_of(s, narrow)

        def send(self, w, sem, device):
            remote(w, w, sem, device).start()
            self.started += 1

        def straight(self, j):
            return has_y and all(order[n][j][0] in ranks[n][rest - STRAIGHT:] for n in self.members) and (
                not crosses or order[self.members[0]][j][1] not in crosses
            )

        def to_core(self, w, slot):
            if has_core:
                self.send(w, c_sem.at[slot], {"wide": base + flip(part, 1)})

        def chain(self, j):
            s, u, slot = self.item(j)
            w = piece_of(s, u)
            await_view(w, z_sem.at[slot, u])
            if 0 not in self.members:
                ahead = jnp.where(s < narrow, narrow + 1, narrow - 1)
                self.send(w, z_sem.at[slot_of(s, ahead), u], {"narrow": ahead})
            if crosses and u >= units:
                self.to_core(w, slot)

        def plane(self, j):
            s, u, slot = self.item(j)
            w = view(s, part, u)
            if has_x:
                self.send(w, x_sem.at[slot, u], {"wide": base + flip(part, 2)})
            if has_y:
                self.send(w, y_sem.at[slot, u], {"wide": base + flip(part, 4)})
            if self.straight(j):
                self.send(w, d_sem.at[slot, u], {"wide": base + flip(part, 6)})
            self.to_core(w, slot)

        def side(self, j):
            s, u, slot = self.item(j)
            odd = (s if crosses else u + jnp.where(u == units - 1, s, 0)) % 2
            for name, mask, sem, there, turn in (("x", 2, x_sem, 4, 0), ("y", 4, y_sem, 2, 1)):
                if mask < pieces:
                    w = view(s, flip(part, mask), u)
                    await_view(w, sem.at[slot, u])
                    if has_y and not (crosses and u in crosses) and not self.straight(j):
                        onward = remote(w, w, d_sem.at[slot, u], {"wide": base + flip(part, there)})

                        @pl.when(odd == turn)
                        def _():
                            onward.start()
                    self.to_core(w, slot)
            if has_y and not (crosses and u in crosses) and not self.straight(j):
                self.started += 1

        def corner(self, j):
            s, u, slot = self.item(j)
            w = view(s, flip(part, 6), u)
            await_view(w, d_sem.at[slot, u])
            self.to_core(w, slot)

        def gathered(self, i):
            s = pick([ranks[n][i] if n in self.members else ranks[self.members[0]][i] for n in range(n_narrow)])
            if has_core:
                await_view(weights.at[pl.ds(0, shard // 2), :], c_sem.at[slot_of(s, narrow)])
            if chunked and i < rest - 1:
                add_chunk(s, False)

        def lookups(self, way):
            d, inner = way
            middle = narrow < n_narrow - 1 - narrow
            up = middle if inner else jnp.logical_not(middle)
            owner = jnp.where(up, narrow + d, narrow - d)
            valid = jnp.logical_and(owner >= 0, owner < n_narrow)
            owner = jnp.where(valid, owner, (narrow + 1) % n_narrow)
            for g in range(groups):
                block = pl.ds(2 * g, 2)
                copy = remote(
                    counts_hbm.at[block, :, lane_block(owner, bags)], looks.at[narrow, block],
                    look_sem.at[g], {"narrow": owner},
                )

                @pl.when(valid)
                def _():
                    copy.start()

        def settle(self):
            most = weights.shape[0] // piece_rows
            count = self.started
            while count > 0:
                k = min(count, most)
                w = weights.at[pl.ds(0, k * piece_rows), pl.ds(0, top)]
                remote(w, w, c_sem.at[0], {"narrow": (narrow + 1) % n_narrow}).wait_send()
                count -= k

    def add_chunk(source, fresh):
        rows = lane_block(source, shard)
        value = jnp.dot(
            pooled[:, rows], weights[rows, pl.ds(0, inner)], preferred_element_type=jnp.float32
        )
        if fresh:
            hidden[...] = value
        else:
            hidden[...] = hidden[...] + value
        back[:, rows] = lax.dot_general(
            cot[...], weights[rows, pl.ds(inner, top)], NT, preferred_element_type=jnp.float32
        )

    chunked = shard % 128 == 0
    for copy in own_x:
        copy.wait()
    if chunked:
        add_chunk(narrow, True)

    roles = [Role([n for n in (0, n_narrow - 1)])]
    if n_narrow > 2:
        roles.append(Role(list(range(1, n_narrow - 1))))
    for r, role in enumerate(roles):
        n = role.members[0]
        plan = []
        at = {}
        placed = 0
        for j, (s, u) in enumerate(order[n]):
            z = HOP_Z * abs(s - n) + STEP_Z * u
            plan.append((z, 0, role.chain, j))
            last = z
            if u < units:
                p = z if r == 0 else max(z, HOP_Z + PACE * placed)
                if role.straight(j):
                    p = max(p, HOP_Z + HOP_S + 0.01)
                placed += 1
                plan.append((p, 1, role.plane, j))
                last = p
                if has_x:
                    last = p + HOP_S
                    plan.append((last, 2, role.side, j))
                if has_y and u not in crosses:
                    last = p + (HOP_W if role.straight(j) else HOP_S + HOP_D)
                    plan.append((last, 3, role.corner, j))
            at[s] = max(last, at.get(s, 0.0))
        done = max(t for t, _, kind, _ in plan if kind == role.chain)
        for d in range(1, n_narrow):
            if r == 0:
                plan.append((0.0 if d == 1 else done + (END_2 if d == 2 else END_3), 1.5, role.lookups, (d, True)))
            else:
                plan.append((done + (MID_1 if d == 1 else MID_2), 1.5, role.lookups, (d, True)))
                plan.append((done + MID_0, 1.5, role.lookups, (d, False)))
        for i in range(rest):
            s = ranks[n][i]
            plan.append((at[s] + HOP_C, 4, role.gathered, i))
        plan.sort(key=lambda e: e[:2])
        kinds = [(e[2], e[3]) for e in plan]
        for j in range(len(order[n])):
            if order[n][j][1] < units and role.straight(j):
                assert kinds.index((role.side, 0)) < kinds.index((role.plane, j))

        @pl.when(jnp.logical_or(narrow == 0, narrow == n_narrow - 1) if r == 0 else jnp.logical_and(narrow > 0, narrow < n_narrow - 1))
        def _():
            for _, _, event, j in plan:
                event(j)

    for copy in own_rest:
        copy.wait()
    tile = min(ACT_TILE, inner)
    if chunked:
        last = lane_block(pick([r[rest - 1] for r in ranks]), shard)
        back[:, last] = lax.dot_general(
            cot[...], weights[last, pl.ds(inner, top)], NT, preferred_element_type=jnp.float32
        )
    for t in range(inner // tile):
        columns = pl.ds(t * tile, tile)
        if chunked:
            value = hidden[:, columns] + jnp.dot(
                pooled[:, last], weights[last, columns], preferred_element_type=jnp.float32
            )
            back_value = back[:, columns]
        else:
            value = jnp.dot(pooled[...], weights[:, columns], preferred_element_type=jnp.float32)
            back_value = lax.dot_general(
                cot[...], weights[columns, pl.ds(inner, top)], NT, preferred_element_type=jnp.float32
            )
        value = value + bias[:, columns]
        sig = jax.nn.sigmoid(value)
        slopes = sig * (1.0 + value * (1.0 - sig))
        deltas[:, columns] = (back_value * slopes).astype(jnp.bfloat16)
    far = [[s for _, s in sorted((-abs(s - n), s) for s in range(n_narrow) if s != n)] for n in range(n_narrow)]
    per_half = groups // HALVES if groups % HALVES == 0 else groups
    for h in range(groups // per_half):
        span = pl.ds(2 * h * per_half * emb, 2 * per_half * emb)
        grad_in[:, span] = lax.dot_general(
            deltas[...], weights[span, pl.ds(0, inner)], NT, preferred_element_type=jnp.float32
        ).astype(jnp.bfloat16)
        for g in range(h * per_half, (h + 1) * per_half):
            await_view(looks.at[pl.ds(0, rest), pl.ds(2 * g, 2)], look_sem.at[g])
        for g in range(h * per_half, (h + 1) * per_half):
            lookups = looks[:, 2 * g:2 * (g + 1)].reshape(n_narrow * 2 * slots, bags)
            value = jnp.dot(
                lookups, grad_in[:, 2 * g * emb:2 * (g + 1) * emb],
                preferred_element_type=jnp.float32,
            )
            value = value.reshape(n_narrow, 2, slots, 2 * emb)
            for i in range(2):
                rows = value[:, i, :, i * emb:(i + 1) * emb]
                gfull[:, 2 * g + i] = rows
                gsend[:, 2 * g + i] = rows.astype(jnp.bfloat16)
        for g in range(h * per_half, (h + 1) * per_half):
            block = pl.ds(2 * g, 2)
            for i in range(rest):
                owner = pick([f[i] for f in far])
                launch(remote(
                    gsend.at[owner, block], grecv.at[slot_of(narrow, owner), block],
                    grad_sem.at[g], {"narrow": owner},
                ))
    for g in range(groups):
        block = pl.ds(2 * g, 2)
        await_view(grecv.at[:, block], grad_sem.at[g])
        total = gfull[narrow, block]
        for d in range(rest):
            total = total + grecv[d, block].astype(jnp.float32)
        grads = total * scale
        norms = jnp.sqrt(jnp.sum(grads * grads, axis=-1, keepdims=True))
        sums[wide, block] = (grads * (limit / jnp.maximum(norms, limit))).astype(jnp.bfloat16)
        for e in range(n_wide - 1, 0, -1):
            peer = base + flip(part, e) if pieces == n_wide else (wide + e) % n_wide
            launch(remote(
                sums.at[wide, block], sums.at[wide, block], sum_sem.at[g], {"wide": peer},
            ))
    for g in range(groups):
        block = pl.ds(2 * g, 2)
        await_view(sums.at[pl.ds(0, n_wide - 1), block], sum_sem.at[g])
        summed = sums[0, block].astype(jnp.float32)
        for q in range(1, n_wide):
            summed = summed + sums[q, block].astype(jnp.float32)
        for i in range(2):
            k = 2 * g + i
            hot = lax.broadcasted_iota(jnp.int32, (out_ref.shape[1], slots), 0) == ids[k:k + 1, :]
            out_ref[k] = jnp.dot(
                hot.astype(jnp.float32), summed[i], precision=lax.Precision.HIGHEST,
                preferred_element_type=jnp.float32,
            )
    for g in range(groups):
        w = looks.at[pl.ds(0, rest), pl.ds(2 * g, 2)]
        remote(w, w, c_sem.at[0], {"narrow": (narrow + 1) % n_narrow}).wait_send()
    for r, role in enumerate(roles):
        @pl.when(jnp.logical_or(narrow == 0, narrow == n_narrow - 1) if r == 0 else jnp.logical_and(narrow > 0, narrow < n_narrow - 1))
        def _():
            role.settle()
    for copy, cond in sent:
        if cond is None:
            copy.wait_send()
        else:
            @pl.when(cond)
            def _():
                copy.wait_send()


def shards(n_wide, n_narrow, pooled, cotangent, w_first, b_first, w_second, counts, row_ids, table, accum):
    tables, slots, group_bags = counts.shape
    emb = table.shape[2]
    bags, emb_all = pooled.shape
    shard, inner = w_first.shape
    top = w_second.shape[1]
    units = inner // top + 1
    pieces = pieces_of(shard, n_wide)
    rest = n_narrow - 1
    groups = tables // 2
    scale = 1.0 / math.sqrt(group_bags)
    limit = clip_factor * math.sqrt(emb)
    hbm = pl.BlockSpec(memory_space=pl.ANY)
    vmem = pl.BlockSpec(memory_space=pltpu.VMEM)
    dma = pltpu.SemaphoreType.DMA
    summed = pl.pallas_call(
        functools.partial(tower_kernel, n_wide, n_narrow, pieces, scale, limit),
        out_shape=jax.ShapeDtypeStruct(table.shape, jnp.float32),
        in_specs=[hbm] * 7,
        out_specs=vmem,
        scratch_shapes=[
            pltpu.VMEM((bags, emb_all), jnp.bfloat16),
            pltpu.VMEM((bags, top), jnp.bfloat16),
            pltpu.VMEM((emb_all, inner + top), jnp.bfloat16),
            pltpu.VMEM((1, inner), jnp.float32),
            pltpu.VMEM(row_ids.shape, jnp.int32),
            pltpu.VMEM((n_narrow, tables, slots, bags), jnp.bfloat16),
            pltpu.VMEM((bags, inner), jnp.float32),
            pltpu.VMEM((bags, inner), jnp.float32),
            pltpu.VMEM((bags, inner), jnp.bfloat16),
            pltpu.VMEM((bags, emb_all), jnp.bfloat16),
            pltpu.VMEM((n_narrow, tables, slots, emb), jnp.float32),
            pltpu.VMEM((n_narrow, tables, slots, emb), jnp.bfloat16),
            pltpu.VMEM((rest, tables, slots, emb), jnp.bfloat16),
            pltpu.VMEM((n_wide, tables, slots, emb), jnp.bfloat16),
            dma((7,)),
            dma,
            dma((rest, units + len(Z_UNITS))),
            dma((rest, units)),
            dma((rest, units)),
            dma((rest, units)),
            dma((rest,)),
            dma((groups,)),
            dma((groups,)),
            dma((groups,)),
        ],
        compiler_params=pltpu.CompilerParams(
            collective_id=0, has_side_effects=True, vmem_limit_bytes=VMEM_KIB * 1024
        ),
        name="tower",
    )(*[
        pltpu.with_memory_space_constraint(x, pltpu.HBM)
        for x in (pooled, cotangent, w_first, w_second, b_first.reshape(1, inner), counts, row_ids)
    ])
    new_accum = accum + summed * summed
    return table - learn_rate * summed / (jnp.sqrt(new_accum) + epsilon), new_accum


def solution(mesh):
    in_specs = (
        P(("wide", "narrow"), None),
        P(("wide", "narrow"), None),
        P("narrow", None),
        P(),
        P("narrow", None),
        P(None, "narrow", "wide"),
        P(None, "narrow"),
        P(None, "narrow", None),
        P(None, "narrow", None),
    )
    out_specs = (P(None, "narrow", None), P(None, "narrow", None))
    step = functools.partial(shards, mesh.shape["wide"], mesh.shape["narrow"])
    return jax.shard_map(step, mesh=mesh, in_specs=in_specs, out_specs=out_specs, check_vma=False)
```

```python
import functools
import math

import jax
import jax.numpy as jnp
from jax import lax
from jax.experimental import pallas as pl
from jax.experimental.pallas import tpu as pltpu
from jax.sharding import PartitionSpec as P

MESH = pl.DeviceIdType.MESH
clip_factor = 0.5
learn_rate = 0.05
epsilon = 1e-08
NT = (((1,), (1,)), ((), ()))
HOP_Z = 3.0
STEP_Z = 0.35 / 2
SPLIT = 2
PACE = 0.0
HOP_S = 3.4
HOP_D = 3.4
HOP_C = 1.4
HOP_W = 4.0
STRAIGHT = 1
END_2 = 0.0
END_3 = 0.0
MID_0 = 0.0
MID_1 = -2.6
MID_2 = 0.0
ACT_TILE = 512
Z_UNITS = (5,)
HALVES = 2
VMEM_KIB = 32 * 1024


def flip(index, mask):
    bit = 1
    while bit <= mask:
        if mask & bit:
            index = index + bit * (1 - 2 * ((index // bit) % 2))
        bit *= 2
    return index


def pieces_of(shard_rows, n_wide):
    pieces = 1
    while pieces < 8 and n_wide % (2 * pieces) == 0 and shard_rows % (32 * pieces) == 0:
        pieces *= 2
    return pieces


def arrivals(n, n_narrow, count):
    items = []
    for s in range(n_narrow):
        if s != n:
            for v in range(count):
                items.append(((abs(s - n) - 1) * count + v, s > n, s, v))
    return [(s, v) for _, _, s, v in sorted(items)]


def tower_kernel(
    n_wide, n_narrow, pieces, scale, limit,
    pooled_hbm, cot_hbm, w1_hbm, w2_hbm, bias_hbm, counts_hbm, ids_hbm, out_ref,
    pooled, cot, weights, bias, ids, looks, hidden, back, deltas, grad_in, gfull, gsend, grecv, sums,
    local_sem, send_sem, z_sem, side_sem, d_sem, c_sem, look_sem, grad_sem, sum_sem,
):
    wide = lax.axis_index("wide")
    narrow = lax.axis_index("narrow")
    shard, inner = w1_hbm.shape
    top = w2_hbm.shape[1]
    width = top // SPLIT
    units = (inner + top) // width
    piece_rows = shard // pieces
    bags = pooled.shape[0]
    emb = gfull.shape[3]
    tables, slots = looks.shape[1], looks.shape[2]
    rest = n_narrow - 1
    part = wide % pieces
    base = wide - part
    has_core, has_x, has_y = pieces >= 2, pieces >= 4, pieces >= 8
    def lane_block(index, size):
        return pl.ds(pl.multiple_of(index * size, size), size)

    def local(step, src, dst):
        return pltpu.make_async_copy(src, dst, local_sem.at[step])

    own_rows = lane_block(narrow, shard)
    own_w = [
        local(0, w1_hbm, weights.at[own_rows, pl.ds(0, inner)]),
        local(1, w2_hbm, weights.at[own_rows, pl.ds(inner, top)]),
    ]
    own_x = [local(2, pooled_hbm, pooled), local(3, cot_hbm, cot)]
    own_rest = [
        local(4, counts_hbm.at[:, :, lane_block(narrow, bags)], looks.at[narrow]),
        local(5, bias_hbm, bias),
        local(6, ids_hbm, ids),
    ]
    for copy in own_w + own_x + own_rest:
        copy.start()

    barrier = pltpu.get_barrier_semaphore()

    def greet(device):
        pl.semaphore_signal(barrier, inc=1, device_id=device, device_id_type=MESH)

    @pl.when(narrow > 0)
    def _():
        greet({"narrow": narrow - 1})

    @pl.when(narrow < n_narrow - 1)
    def _():
        greet({"narrow": narrow + 1})

    if pieces == n_wide:
        beside = [base + flip(part, m) for m in (1, 2, 4) if m < pieces]
    else:
        beside = [(wide + d) % n_wide for d in range(1, n_wide)]
    for device in beside:
        greet({"wide": device})
    ends = jnp.where(narrow > 0, 1, 0) + jnp.where(narrow < n_narrow - 1, 1, 0)
    pl.semaphore_wait(barrier, ends + len(beside))

    def remote(src, dst, recv, device):
        return pltpu.make_async_remote_copy(
            src_ref=src, dst_ref=dst, send_sem=send_sem, recv_sem=recv,
            device_id=device, device_id_type=MESH,
        )

    sent = []

    def launch(copy, cond=None):
        if cond is None:
            copy.start()
        else:
            @pl.when(cond)
            def _():
                copy.start()
        sent.append((copy, cond))

    def pick(values):
        if all(v == values[0] for v in values):
            return values[0]
        total = 0
        for n, v in enumerate(values):
            total = total + jnp.where(narrow == n, v, 0)
        return total

    def slot_of(s, n):
        return (s - n + n_narrow) % n_narrow - 1

    def view(s, q, u):
        rows = pl.ds(pl.multiple_of(s * shard + q * piece_rows, piece_rows), piece_rows)
        return weights.at[rows, lane_block(u, width)]

    crosses = [u for u in range(units) if has_y and n_narrow <= 4 and u in Z_UNITS]

    def piece_of(s, v):
        if crosses and v >= units:
            return view(s, flip(part, 6), crosses[v - units])
        return view(s, part, v)

    for copy in own_w:
        copy.wait()
    for v in range(units + len(crosses)):
        w = piece_of(narrow, v)
        for ahead, cond in ((narrow + 1, narrow < n_narrow - 1), (narrow - 1, narrow > 0)):
            launch(remote(w, w, z_sem.at[slot_of(narrow, ahead), v], {"narrow": ahead}), cond)

    order = [arrivals(n, n_narrow, units + len(crosses)) for n in range(n_narrow)]
    groups = tables // 2
    ranks = [sorted((s for s in range(n_narrow) if s != n), key=lambda s: (abs(s - n), s > n)) for n in range(n_narrow)]

    def await_view(w, sem):
        remote(w, w, sem, {"narrow": (narrow + 1) % n_narrow}).wait_recv()

    class Role:
        def __init__(self, members):
            self.members = members
            self.started = 0
            self.looks = 0

        def item(self, j):
            pairs = [order[n][j] if n in self.members else (-1, -1) for n in range(n_narrow)]
            fill = order[self.members[0]][j]
            pairs = [fill if p[0] < 0 else p for p in pairs]
            s, u = pick([p[0] for p in pairs]), pick([p[1] for p in pairs])
            assert not crosses or isinstance(u, int)
            return s, u, slot_of(s, narrow)

        def send(self, w, sem, device):
            remote(w, w, sem, device).start()
            self.started += 1

        def straight(self, j):
            return has_y and all(order[n][j][0] in ranks[n][rest - STRAIGHT:] for n in self.members) and (
                not crosses or order[self.members[0]][j][1] not in crosses
            )

        def to_core(self, w, slot):
            if has_core:
                self.send(w, c_sem.at[slot], {"wide": base + flip(part, 1)})

        def chain(self, j):
            s, u, slot = self.item(j)
            w = piece_of(s, u)
            await_view(w, z_sem.at[slot, u])
            if 0 not in self.members:
                ahead = jnp.where(s < narrow, narrow + 1, narrow - 1)
                self.send(w, z_sem.at[slot_of(s, ahead), u], {"narrow": ahead})
            if crosses and u >= units:
                self.to_core(w, slot)

        def plane(self, j):
            s, u, slot = self.item(j)
            w = view(s, part, u)
            if has_x:
                self.send(w, side_sem.at[slot, u], {"wide": base + flip(part, 2)})
            if has_y:
                self.send(w, side_sem.at[slot, u], {"wide": base + flip(part, 4)})
            if self.straight(j):
                self.send(w, d_sem.at[slot, u], {"wide": base + flip(part, 6)})
            self.to_core(w, slot)

        def side(self, j):
            s, u, slot = self.item(j)
            odd = (s + u if crosses else u + jnp.where(u == units - 1, s, 0)) % 2
            beside = 2 if has_y else 1
            await_view(weights.at[pl.ds(0, beside * piece_rows), lane_block(u, width)], side_sem.at[slot, u])
            for mask, there, turn in ((2, 4, 0), (4, 2, 1)):
                if mask < pieces:
                    w = view(s, flip(part, mask), u)
                    if has_y and not (crosses and u in crosses) and not self.straight(j):
                        onward = remote(w, w, d_sem.at[slot, u], {"wide": base + flip(part, there)})

                        @pl.when(odd == turn)
                        def _():
                            onward.start()
                    self.to_core(w, slot)
            if has_y and not (crosses and u in crosses) and not self.straight(j):
                self.started += 1

        def corner(self, j):
            s, u, slot = self.item(j)
            w = view(s, flip(part, 6), u)
            await_view(w, d_sem.at[slot, u])
            self.to_core(w, slot)

        def gathered(self, i):
            s = pick([ranks[n][i] if n in self.members else ranks[self.members[0]][i] for n in range(n_narrow)])
            if has_core:
                await_view(weights.at[pl.ds(0, shard // 2), :], c_sem.at[slot_of(s, narrow)])
            if chunked and i < rest - 1:
                add_chunk(s, False)

        def lookups(self, way):
            d, inner = way
            middle = narrow < n_narrow - 1 - narrow
            up = middle if inner else jnp.logical_not(middle)
            owner = jnp.where(up, narrow + d, narrow - d)
            valid = jnp.logical_and(owner >= 0, owner < n_narrow)
            owner = jnp.where(valid, owner, (narrow + 1) % n_narrow)
            for g in range(groups):
                block = pl.ds(2 * g, 2)
                copy = remote(
                    counts_hbm.at[block, :, lane_block(owner, bags)], looks.at[narrow, block],
                    look_sem.at[g], {"narrow": owner},
                )

                @pl.when(valid)
                def _():
                    copy.start()

        def settle(self):
            most = weights.shape[0] // piece_rows
            count = self.started
            while count > 0:
                k = min(count, most)
                w = weights.at[pl.ds(0, k * piece_rows), pl.ds(0, width)]
                remote(w, w, c_sem.at[0], {"narrow": (narrow + 1) % n_narrow}).wait_send()
                count -= k

    def add_chunk(source, fresh):
        rows = lane_block(source, shard)
        value = jnp.dot(
            pooled[:, rows], weights[rows, pl.ds(0, inner)], preferred_element_type=jnp.float32
        )
        if fresh:
            hidden[...] = value
        else:
            hidden[...] = hidden[...] + value
        back[:, rows] = lax.dot_general(
            cot[...], weights[rows, pl.ds(inner, top)], NT, preferred_element_type=jnp.float32
        )

    chunked = shard % 128 == 0
    for copy in own_x:
        copy.wait()
    if chunked:
        add_chunk(narrow, True)

    roles = [Role([n for n in (0, n_narrow - 1)])]
    if n_narrow > 2:
        roles.append(Role(list(range(1, n_narrow - 1))))
    for r, role in enumerate(roles):
        n = role.members[0]
        plan = []
        at = {}
        placed = 0
        for j, (s, u) in enumerate(order[n]):
            z = HOP_Z * abs(s - n) + STEP_Z * u
            plan.append((z, 0, role.chain, j))
            last = z
            if u < units:
                p = z if r == 0 else max(z, HOP_Z + PACE * placed)
                if role.straight(j):
                    p = max(p, HOP_Z + HOP_S + 0.01)
                placed += 1
                plan.append((p, 1, role.plane, j))
                last = p
                if has_x:
                    last = p + HOP_S
                    plan.append((last, 2, role.side, j))
                if has_y and u not in crosses:
                    last = p + (HOP_W if role.straight(j) else HOP_S + HOP_D)
                    plan.append((last, 3, role.corner, j))
            at[s] = max(last, at.get(s, 0.0))
        done = max(t for t, _, kind, _ in plan if kind == role.chain)
        for d in range(1, n_narrow):
            if r == 0:
                plan.append((0.0 if d == 1 else done + (END_2 if d == 2 else END_3), 1.5, role.lookups, (d, True)))
            else:
                plan.append((done + (MID_1 if d == 1 else MID_2), 1.5, role.lookups, (d, True)))
                plan.append((done + MID_0, 1.5, role.lookups, (d, False)))
        for i in range(rest):
            s = ranks[n][i]
            plan.append((at[s] + HOP_C, 4, role.gathered, i))
        plan.sort(key=lambda e: e[:2])
        kinds = [(e[2], e[3]) for e in plan]
        for j in range(len(order[n])):
            if order[n][j][1] < units and role.straight(j):
                assert kinds.index((role.side, 0)) < kinds.index((role.plane, j))

        @pl.when(jnp.logical_or(narrow == 0, narrow == n_narrow - 1) if r == 0 else jnp.logical_and(narrow > 0, narrow < n_narrow - 1))
        def _():
            for _, _, event, j in plan:
                event(j)

    for copy in own_rest:
        copy.wait()
    tile = min(ACT_TILE, inner)
    if chunked:
        last = lane_block(pick([r[rest - 1] for r in ranks]), shard)
        back[:, last] = lax.dot_general(
            cot[...], weights[last, pl.ds(inner, top)], NT, preferred_element_type=jnp.float32
        )
    for t in range(inner // tile):
        columns = pl.ds(t * tile, tile)
        if chunked:
            value = hidden[:, columns] + jnp.dot(
                pooled[:, last], weights[last, columns], preferred_element_type=jnp.float32
            )
            back_value = back[:, columns]
        else:
            value = jnp.dot(pooled[...], weights[:, columns], preferred_element_type=jnp.float32)
            back_value = lax.dot_general(
                cot[...], weights[columns, pl.ds(inner, top)], NT, preferred_element_type=jnp.float32
            )
        value = value + bias[:, columns]
        sig = jax.nn.sigmoid(value)
        slopes = sig * (1.0 + value * (1.0 - sig))
        deltas[:, columns] = (back_value * slopes).astype(jnp.bfloat16)
    far = [[s for _, s in sorted((-abs(s - n), s) for s in range(n_narrow) if s != n)] for n in range(n_narrow)]
    per_half = groups // HALVES if groups % HALVES == 0 else groups
    for h in range(groups // per_half):
        span = pl.ds(2 * h * per_half * emb, 2 * per_half * emb)
        grad_in[:, span] = lax.dot_general(
            deltas[...], weights[span, pl.ds(0, inner)], NT, preferred_element_type=jnp.float32
        ).astype(jnp.bfloat16)
        for g in range(h * per_half, (h + 1) * per_half):
            await_view(looks.at[pl.ds(0, rest), pl.ds(2 * g, 2)], look_sem.at[g])
        for g in range(h * per_half, (h + 1) * per_half):
            lookups = looks[:, 2 * g:2 * (g + 1)].reshape(n_narrow * 2 * slots, bags)
            value = jnp.dot(
                lookups, grad_in[:, 2 * g * emb:2 * (g + 1) * emb],
                preferred_element_type=jnp.float32,
            )
            value = value.reshape(n_narrow, 2, slots, 2 * emb)
            for i in range(2):
                rows = value[:, i, :, i * emb:(i + 1) * emb]
                gfull[:, 2 * g + i] = rows
                gsend[:, 2 * g + i] = rows.astype(jnp.bfloat16)
        for g in range(h * per_half, (h + 1) * per_half):
            block = pl.ds(2 * g, 2)
            for i in range(rest):
                owner = pick([f[i] for f in far])
                launch(remote(
                    gsend.at[owner, block], grecv.at[slot_of(narrow, owner), block],
                    grad_sem.at[g], {"narrow": owner},
                ))
    for g in range(groups):
        block = pl.ds(2 * g, 2)
        await_view(grecv.at[:, block], grad_sem.at[g])
        total = gfull[narrow, block]
        for d in range(rest):
            total = total + grecv[d, block].astype(jnp.float32)
        grads = total * scale
        norms = jnp.sqrt(jnp.sum(grads * grads, axis=-1, keepdims=True))
        sums[wide, block] = (grads * (limit / jnp.maximum(norms, limit))).astype(jnp.bfloat16)
        for e in range(n_wide - 1, 0, -1):
            peer = base + flip(part, e) if pieces == n_wide else (wide + e) % n_wide
            launch(remote(
                sums.at[wide, block], sums.at[wide, block], sum_sem.at[g], {"wide": peer},
            ))
    for g in range(groups):
        block = pl.ds(2 * g, 2)
        await_view(sums.at[pl.ds(0, n_wide - 1), block], sum_sem.at[g])
        summed = sums[0, block].astype(jnp.float32)
        for q in range(1, n_wide):
            summed = summed + sums[q, block].astype(jnp.float32)
        for i in range(2):
            k = 2 * g + i
            hot = lax.broadcasted_iota(jnp.int32, (out_ref.shape[1], slots), 0) == ids[k:k + 1, :]
            out_ref[k] = jnp.dot(
                hot.astype(jnp.float32), summed[i], precision=lax.Precision.HIGHEST,
                preferred_element_type=jnp.float32,
            )
    for g in range(groups):
        w = looks.at[pl.ds(0, rest), pl.ds(2 * g, 2)]
        remote(w, w, c_sem.at[0], {"narrow": (narrow + 1) % n_narrow}).wait_send()
    for r, role in enumerate(roles):
        @pl.when(jnp.logical_or(narrow == 0, narrow == n_narrow - 1) if r == 0 else jnp.logical_and(narrow > 0, narrow < n_narrow - 1))
        def _():
            role.settle()
    for copy, cond in sent:
        if cond is None:
            copy.wait_send()
        else:
            @pl.when(cond)
            def _():
                copy.wait_send()


def shards(n_wide, n_narrow, pooled, cotangent, w_first, b_first, w_second, counts, row_ids, table, accum):
    tables, slots, group_bags = counts.shape
    emb = table.shape[2]
    bags, emb_all = pooled.shape
    shard, inner = w_first.shape
    top = w_second.shape[1]
    width = top // SPLIT
    units = (inner + top) // width
    pieces = pieces_of(shard, n_wide)
    rest = n_narrow - 1
    groups = tables // 2
    scale = 1.0 / math.sqrt(group_bags)
    limit = clip_factor * math.sqrt(emb)
    hbm = pl.BlockSpec(memory_space=pl.ANY)
    vmem = pl.BlockSpec(memory_space=pltpu.VMEM)
    dma = pltpu.SemaphoreType.DMA
    summed = pl.pallas_call(
        functools.partial(tower_kernel, n_wide, n_narrow, pieces, scale, limit),
        out_shape=jax.ShapeDtypeStruct(table.shape, jnp.float32),
        in_specs=[hbm] * 7,
        out_specs=vmem,
        scratch_shapes=[
            pltpu.VMEM((bags, emb_all), jnp.bfloat16),
            pltpu.VMEM((bags, top), jnp.bfloat16),
            pltpu.VMEM((emb_all, inner + top), jnp.bfloat16),
            pltpu.VMEM((1, inner), jnp.float32),
            pltpu.VMEM(row_ids.shape, jnp.int32),
            pltpu.VMEM((n_narrow, tables, slots, bags), jnp.bfloat16),
            pltpu.VMEM((bags, inner), jnp.float32),
            pltpu.VMEM((bags, inner), jnp.float32),
            pltpu.VMEM((bags, inner), jnp.bfloat16),
            pltpu.VMEM((bags, emb_all), jnp.bfloat16),
            pltpu.VMEM((n_narrow, tables, slots, emb), jnp.float32),
            pltpu.VMEM((n_narrow, tables, slots, emb), jnp.bfloat16),
            pltpu.VMEM((rest, tables, slots, emb), jnp.bfloat16),
            pltpu.VMEM((n_wide, tables, slots, emb), jnp.bfloat16),
            dma((7,)),
            dma,
            dma((rest, units + len(Z_UNITS))),
            dma((rest, units)),
            dma((rest, units)),
            dma((rest,)),
            dma((groups,)),
            dma((groups,)),
            dma((groups,)),
        ],
        compiler_params=pltpu.CompilerParams(
            collective_id=0, has_side_effects=True, vmem_limit_bytes=VMEM_KIB * 1024
        ),
        name="tower",
    )(*[
        pltpu.with_memory_space_constraint(x, pltpu.HBM)
        for x in (pooled, cotangent, w_first, w_second, b_first.reshape(1, inner), counts, row_ids)
    ])
    new_accum = accum + summed * summed
    return table - learn_rate * summed / (jnp.sqrt(new_accum) + epsilon), new_accum


def solution(mesh):
    in_specs = (
        P(("wide", "narrow"), None),
        P(("wide", "narrow"), None),
        P("narrow", None),
        P(),
        P("narrow", None),
        P(None, "narrow", "wide"),
        P(None, "narrow"),
        P(None, "narrow", None),
        P(None, "narrow", None),
    )
    out_specs = (P(None, "narrow", None), P(None, "narrow", None))
    step = functools.partial(shards, mesh.shape["wide"], mesh.shape["narrow"])
    return jax.shard_map(step, mesh=mesh, in_specs=in_specs, out_specs=out_specs, check_vma=False)
```

```python
import functools
import math

import jax
import jax.numpy as jnp
from jax import lax
from jax.experimental import pallas as pl
from jax.experimental.pallas import tpu as pltpu
from jax.sharding import PartitionSpec as P

MESH = pl.DeviceIdType.MESH
clip_factor = 0.5
learn_rate = 0.05
epsilon = 1e-08
NT = (((1,), (1,)), ((), ()))
HOP_Z = 3.0
STEP_Z = 0.35 / 2
SPLIT = 2
PACE = 0.0
HOP_S = 3.4
HOP_D = 3.4
HOP_C = 1.4
HOP_W = 3.4
STRAIGHT = 1
END_2 = 0.0
END_3 = 0.0
MID_0 = 0.0
MID_1 = -2.6
MID_2 = 0.0
ACT_TILE = 1024
Z_UNITS = (5,)
HALVES = 2
VMEM_KIB = 32 * 1024


def flip(index, mask):
    bit = 1
    while bit <= mask:
        if mask & bit:
            index = index + bit * (1 - 2 * ((index // bit) % 2))
        bit *= 2
    return index


def pieces_of(shard_rows, n_wide):
    pieces = 1
    while pieces < 8 and n_wide % (2 * pieces) == 0 and shard_rows % (32 * pieces) == 0:
        pieces *= 2
    return pieces


def arrivals(n, n_narrow, count):
    items = []
    for s in range(n_narrow):
        if s != n:
            for v in range(count):
                items.append(((abs(s - n) - 1) * count + v, s > n, s, v))
    return [(s, v) for _, _, s, v in sorted(items)]


def tower_kernel(
    n_wide, n_narrow, pieces, scale, limit,
    pooled_hbm, cot_hbm, w1_hbm, w2_hbm, bias_hbm, counts_hbm, ids_hbm, out_ref,
    pooled, cot, weights, bias, ids, looks, hidden, back, deltas, grad_in, gfull, gsend, grecv, sums,
    local_sem, send_sem, z_sem, side_sem, d_sem, c_sem, look_sem, grad_sem, sum_sem,
):
    wide = lax.axis_index("wide")
    narrow = lax.axis_index("narrow")
    shard, inner = w1_hbm.shape
    top = w2_hbm.shape[1]
    width = top // SPLIT
    units = (inner + top) // width
    piece_rows = shard // pieces
    bags = pooled.shape[0]
    emb = gfull.shape[3]
    tables, slots = looks.shape[1], looks.shape[2]
    rest = n_narrow - 1
    part = wide % pieces
    base = wide - part
    has_core, has_x, has_y = pieces >= 2, pieces >= 4, pieces >= 8
    def lane_block(index, size):
        return pl.ds(pl.multiple_of(index * size, size), size)

    def local(step, src, dst):
        return pltpu.make_async_copy(src, dst, local_sem.at[step])

    own_rows = lane_block(narrow, shard)
    own_w = [
        local(0, w1_hbm, weights.at[own_rows, pl.ds(0, inner)]),
        local(1, w2_hbm, weights.at[own_rows, pl.ds(inner, top)]),
    ]
    own_x = [local(2, pooled_hbm, pooled), local(3, cot_hbm, cot)]
    own_rest = [
        local(4, counts_hbm.at[:, :, lane_block(narrow, bags)], looks.at[narrow]),
        local(5, bias_hbm, bias),
        local(6, ids_hbm, ids),
    ]
    for copy in own_w + own_x + own_rest:
        copy.start()

    barrier = pltpu.get_barrier_semaphore()

    def greet(device):
        pl.semaphore_signal(barrier, inc=1, device_id=device, device_id_type=MESH)

    @pl.when(narrow > 0)
    def _():
        greet({"narrow": narrow - 1})

    @pl.when(narrow < n_narrow - 1)
    def _():
        greet({"narrow": narrow + 1})

    if pieces == n_wide:
        beside = [base + flip(part, m) for m in (1, 2, 4) if m < pieces]
    else:
        beside = [(wide + d) % n_wide for d in range(1, n_wide)]
    for device in beside:
        greet({"wide": device})
    ends = jnp.where(narrow > 0, 1, 0) + jnp.where(narrow < n_narrow - 1, 1, 0)
    pl.semaphore_wait(barrier, ends + len(beside))

    def remote(src, dst, recv, device):
        return pltpu.make_async_remote_copy(
            src_ref=src, dst_ref=dst, send_sem=send_sem, recv_sem=recv,
            device_id=device, device_id_type=MESH,
        )

    sent = []

    def launch(copy, cond=None):
        if cond is None:
            copy.start()
        else:
            @pl.when(cond)
            def _():
                copy.start()
        sent.append((copy, cond))

    def pick(values):
        if all(v == values[0] for v in values):
            return values[0]
        total = 0
        for n, v in enumerate(values):
            total = total + jnp.where(narrow == n, v, 0)
        return total

    def slot_of(s, n):
        return (s - n + n_narrow) % n_narrow - 1

    def view(s, q, u):
        rows = pl.ds(pl.multiple_of(s * shard + q * piece_rows, piece_rows), piece_rows)
        return weights.at[rows, lane_block(u, width)]

    crosses = [u for u in range(units) if has_y and n_narrow <= 4 and u in Z_UNITS]

    def piece_of(s, v):
        if crosses and v >= units:
            return view(s, flip(part, 6), crosses[v - units])
        return view(s, part, v)

    for copy in own_w:
        copy.wait()
    for v in range(units + len(crosses)):
        w = piece_of(narrow, v)
        for ahead, cond in ((narrow + 1, narrow < n_narrow - 1), (narrow - 1, narrow > 0)):
            launch(remote(w, w, z_sem.at[slot_of(narrow, ahead), v], {"narrow": ahead}), cond)

    order = [arrivals(n, n_narrow, units + len(crosses)) for n in range(n_narrow)]
    groups = tables // 2
    ranks = [sorted((s for s in range(n_narrow) if s != n), key=lambda s: (abs(s - n), s > n)) for n in range(n_narrow)]

    def await_view(w, sem):
        remote(w, w, sem, {"narrow": (narrow + 1) % n_narrow}).wait_recv()

    class Role:
        def __init__(self, members):
            self.members = members
            self.started = 0
            self.looks = 0

        def item(self, j):
            pairs = [order[n][j] if n in self.members else (-1, -1) for n in range(n_narrow)]
            fill = order[self.members[0]][j]
            pairs = [fill if p[0] < 0 else p for p in pairs]
            s, u = pick([p[0] for p in pairs]), pick([p[1] for p in pairs])
            assert not crosses or isinstance(u, int)
            return s, u, slot_of(s, narrow)

        def send(self, w, sem, device):
            remote(w, w, sem, device).start()
            self.started += 1

        def straight(self, j):
            return has_y and all(order[n][j][0] in ranks[n][rest - STRAIGHT:] for n in self.members) and (
                not crosses or order[self.members[0]][j][1] not in crosses
            )

        def to_core(self, w, slot):
            if has_core:
                self.send(w, c_sem.at[slot], {"wide": base + flip(part, 1)})

        def chain(self, j):
            s, u, slot = self.item(j)
            w = piece_of(s, u)
            await_view(w, z_sem.at[slot, u])
            if 0 not in self.members:
                ahead = jnp.where(s < narrow, narrow + 1, narrow - 1)
                self.send(w, z_sem.at[slot_of(s, ahead), u], {"narrow": ahead})
            if crosses and u >= units:
                self.to_core(w, slot)

        def plane(self, j):
            s, u, slot = self.item(j)
            w = view(s, part, u)
            if has_x:
                self.send(w, side_sem.at[slot, u], {"wide": base + flip(part, 2)})
            if has_y:
                self.send(w, side_sem.at[slot, u], {"wide": base + flip(part, 4)})
            if self.straight(j):
                self.send(w, d_sem.at[slot, u], {"wide": base + flip(part, 6)})
            self.to_core(w, slot)

        def side(self, j):
            s, u, slot = self.item(j)
            odd = (s + u if crosses else u + jnp.where(u == units - 1, s, 0)) % 2
            beside = 2 if has_y else 1
            await_view(weights.at[pl.ds(0, beside * piece_rows), lane_block(u, width)], side_sem.at[slot, u])
            for mask, there, turn in ((2, 4, 0), (4, 2, 1)):
                if mask < pieces:
                    w = view(s, flip(part, mask), u)
                    if has_y and not (crosses and u in crosses) and not self.straight(j):
                        onward = remote(w, w, d_sem.at[slot, u], {"wide": base + flip(part, there)})

                        @pl.when(odd == turn)
                        def _():
                            onward.start()
                    self.to_core(w, slot)
            if has_y and not (crosses and u in crosses) and not self.straight(j):
                self.started += 1

        def corner(self, j):
            s, u, slot = self.item(j)
            w = view(s, flip(part, 6), u)
            await_view(w, d_sem.at[slot, u])
            self.to_core(w, slot)

        def gathered(self, i):
            s = pick([ranks[n][i] if n in self.members else ranks[self.members[0]][i] for n in range(n_narrow)])
            if has_core:
                await_view(weights.at[pl.ds(0, shard // 2), :], c_sem.at[slot_of(s, narrow)])
            if chunked and i < rest - 1:
                add_chunk(s, False)

        def lookups(self, way):
            d, inner = way
            middle = narrow < n_narrow - 1 - narrow
            up = middle if inner else jnp.logical_not(middle)
            owner = jnp.where(up, narrow + d, narrow - d)
            valid = jnp.logical_and(owner >= 0, owner < n_narrow)
            owner = jnp.where(valid, owner, (narrow + 1) % n_narrow)
            for g in range(groups):
                block = pl.ds(2 * g, 2)
                copy = remote(
                    counts_hbm.at[block, :, lane_block(owner, bags)], looks.at[narrow, block],
                    look_sem.at[g], {"narrow": owner},
                )

                @pl.when(valid)
                def _():
                    copy.start()

        def settle(self):
            most = weights.shape[0] // piece_rows
            count = self.started
            while count > 0:
                k = min(count, most)
                w = weights.at[pl.ds(0, k * piece_rows), pl.ds(0, width)]
                remote(w, w, c_sem.at[0], {"narrow": (narrow + 1) % n_narrow}).wait_send()
                count -= k

    def add_chunk(source, fresh):
        rows = lane_block(source, shard)
        value = jnp.dot(
            pooled[:, rows], weights[rows, pl.ds(0, inner)], preferred_element_type=jnp.float32
        )
        if fresh:
            hidden[...] = value
        else:
            hidden[...] = hidden[...] + value
        back[:, rows] = lax.dot_general(
            cot[...], weights[rows, pl.ds(inner, top)], NT, preferred_element_type=jnp.float32
        )

    chunked = shard % 128 == 0
    for copy in own_x:
        copy.wait()
    if chunked:
        add_chunk(narrow, True)

    roles = [Role([n for n in (0, n_narrow - 1)])]
    if n_narrow > 2:
        roles.append(Role(list(range(1, n_narrow - 1))))
    for r, role in enumerate(roles):
        n = role.members[0]
        plan = []
        at = {}
        placed = 0
        for j, (s, u) in enumerate(order[n]):
            z = HOP_Z * abs(s - n) + STEP_Z * u
            plan.append((z, 0, role.chain, j))
            last = z
            if u < units:
                p = z if r == 0 else max(z, HOP_Z + PACE * placed)
                if role.straight(j):
                    p = max(p, HOP_Z + HOP_S + 0.01)
                placed += 1
                plan.append((p, 1, role.plane, j))
                last = p
                if has_x:
                    last = p + HOP_S
                    plan.append((last, 2, role.side, j))
                if has_y and u not in crosses:
                    last = p + (HOP_W if role.straight(j) else HOP_S + HOP_D)
                    plan.append((last, 3, role.corner, j))
            at[s] = max(last, at.get(s, 0.0))
        done = max(t for t, _, kind, _ in plan if kind == role.chain)
        for d in range(1, n_narrow):
            if r == 0:
                plan.append((0.0 if d == 1 else done + (END_2 if d == 2 else END_3), 1.5, role.lookups, (d, True)))
            else:
                plan.append((done + (MID_1 if d == 1 else MID_2), 1.5, role.lookups, (d, True)))
                plan.append((done + MID_0, 1.5, role.lookups, (d, False)))
        for i in range(rest):
            s = ranks[n][i]
            plan.append((at[s] + HOP_C, 4, role.gathered, i))
        plan.sort(key=lambda e: e[:2])
        kinds = [(e[2], e[3]) for e in plan]
        for j in range(len(order[n])):
            if order[n][j][1] < units and role.straight(j):
                assert kinds.index((role.side, 0)) < kinds.index((role.plane, j))

        @pl.when(jnp.logical_or(narrow == 0, narrow == n_narrow - 1) if r == 0 else jnp.logical_and(narrow > 0, narrow < n_narrow - 1))
        def _():
            for _, _, event, j in plan:
                event(j)

    for copy in own_rest:
        copy.wait()
    tile = min(ACT_TILE, inner)
    if chunked:
        last = lane_block(pick([r[rest - 1] for r in ranks]), shard)
        back[:, last] = lax.dot_general(
            cot[...], weights[last, pl.ds(inner, top)], NT, preferred_element_type=jnp.float32
        )
    for t in range(inner // tile):
        columns = pl.ds(t * tile, tile)
        if chunked:
            value = hidden[:, columns] + jnp.dot(
                pooled[:, last], weights[last, columns], preferred_element_type=jnp.float32
            )
            back_value = back[:, columns]
        else:
            value = jnp.dot(pooled[...], weights[:, columns], preferred_element_type=jnp.float32)
            back_value = lax.dot_general(
                cot[...], weights[columns, pl.ds(inner, top)], NT, preferred_element_type=jnp.float32
            )
        value = value + bias[:, columns]
        sig = jax.nn.sigmoid(value)
        slopes = sig * (1.0 + value * (1.0 - sig))
        deltas[:, columns] = (back_value * slopes).astype(jnp.bfloat16)
    far = [[s for _, s in sorted((-abs(s - n), s) for s in range(n_narrow) if s != n)] for n in range(n_narrow)]
    per_half = groups // HALVES if groups % HALVES == 0 else groups
    for h in range(groups // per_half):
        span = pl.ds(2 * h * per_half * emb, 2 * per_half * emb)
        grad_in[:, span] = lax.dot_general(
            deltas[...], weights[span, pl.ds(0, inner)], NT, preferred_element_type=jnp.float32
        ).astype(jnp.bfloat16)
        for g in range(h * per_half, (h + 1) * per_half):
            await_view(looks.at[pl.ds(0, rest), pl.ds(2 * g, 2)], look_sem.at[g])
        for g in range(h * per_half, (h + 1) * per_half):
            lookups = looks[:, 2 * g:2 * (g + 1)].reshape(n_narrow * 2 * slots, bags)
            value = jnp.dot(
                lookups, grad_in[:, 2 * g * emb:2 * (g + 1) * emb],
                preferred_element_type=jnp.float32,
            )
            value = value.reshape(n_narrow, 2, slots, 2 * emb)
            for i in range(2):
                rows = value[:, i, :, i * emb:(i + 1) * emb]
                gfull[:, 2 * g + i] = rows
                gsend[:, 2 * g + i] = rows.astype(jnp.bfloat16)
        for g in range(h * per_half, (h + 1) * per_half):
            block = pl.ds(2 * g, 2)
            for i in range(rest):
                owner = pick([f[i] for f in far])
                launch(remote(
                    gsend.at[owner, block], grecv.at[slot_of(narrow, owner), block],
                    grad_sem.at[g], {"narrow": owner},
                ))
    for g in range(groups):
        block = pl.ds(2 * g, 2)
        await_view(grecv.at[:, block], grad_sem.at[g])
        total = gfull[narrow, block]
        for d in range(rest):
            total = total + grecv[d, block].astype(jnp.float32)
        grads = total * scale
        norms = jnp.sqrt(jnp.sum(grads * grads, axis=-1, keepdims=True))
        sums[wide, block] = (grads * (limit / jnp.maximum(norms, limit))).astype(jnp.bfloat16)
        for e in range(n_wide - 1, 0, -1):
            peer = base + flip(part, e) if pieces == n_wide else (wide + e) % n_wide
            launch(remote(
                sums.at[wide, block], sums.at[wide, block], sum_sem.at[g], {"wide": peer},
            ))
    for g in range(groups):
        block = pl.ds(2 * g, 2)
        await_view(sums.at[pl.ds(0, n_wide - 1), block], sum_sem.at[g])
        summed = sums[0, block].astype(jnp.float32)
        for q in range(1, n_wide):
            summed = summed + sums[q, block].astype(jnp.float32)
        for i in range(2):
            k = 2 * g + i
            hot = lax.broadcasted_iota(jnp.int32, (out_ref.shape[1], slots), 0) == ids[k:k + 1, :]
            out_ref[k] = jnp.dot(
                hot.astype(jnp.float32), summed[i], precision=lax.Precision.HIGHEST,
                preferred_element_type=jnp.float32,
            )
    for g in range(groups):
        w = looks.at[pl.ds(0, rest), pl.ds(2 * g, 2)]
        remote(w, w, c_sem.at[0], {"narrow": (narrow + 1) % n_narrow}).wait_send()
    for r, role in enumerate(roles):
        @pl.when(jnp.logical_or(narrow == 0, narrow == n_narrow - 1) if r == 0 else jnp.logical_and(narrow > 0, narrow < n_narrow - 1))
        def _():
            role.settle()
    for copy, cond in sent:
        if cond is None:
            copy.wait_send()
        else:
            @pl.when(cond)
            def _():
                copy.wait_send()


def shards(n_wide, n_narrow, pooled, cotangent, w_first, b_first, w_second, counts, row_ids, table, accum):
    tables, slots, group_bags = counts.shape
    emb = table.shape[2]
    bags, emb_all = pooled.shape
    shard, inner = w_first.shape
    top = w_second.shape[1]
    width = top // SPLIT
    units = (inner + top) // width
    pieces = pieces_of(shard, n_wide)
    rest = n_narrow - 1
    groups = tables // 2
    scale = 1.0 / math.sqrt(group_bags)
    limit = clip_factor * math.sqrt(emb)
    hbm = pl.BlockSpec(memory_space=pl.ANY)
    vmem = pl.BlockSpec(memory_space=pltpu.VMEM)
    dma = pltpu.SemaphoreType.DMA
    summed = pl.pallas_call(
        functools.partial(tower_kernel, n_wide, n_narrow, pieces, scale, limit),
        out_shape=jax.ShapeDtypeStruct(table.shape, jnp.float32),
        in_specs=[hbm] * 7,
        out_specs=vmem,
        scratch_shapes=[
            pltpu.VMEM((bags, emb_all), jnp.bfloat16),
            pltpu.VMEM((bags, top), jnp.bfloat16),
            pltpu.VMEM((emb_all, inner + top), jnp.bfloat16),
            pltpu.VMEM((1, inner), jnp.float32),
            pltpu.VMEM(row_ids.shape, jnp.int32),
            pltpu.VMEM((n_narrow, tables, slots, bags), jnp.bfloat16),
            pltpu.VMEM((bags, inner), jnp.float32),
            pltpu.VMEM((bags, inner), jnp.float32),
            pltpu.VMEM((bags, inner), jnp.bfloat16),
            pltpu.VMEM((bags, emb_all), jnp.bfloat16),
            pltpu.VMEM((n_narrow, tables, slots, emb), jnp.float32),
            pltpu.VMEM((n_narrow, tables, slots, emb), jnp.bfloat16),
            pltpu.VMEM((rest, tables, slots, emb), jnp.bfloat16),
            pltpu.VMEM((n_wide, tables, slots, emb), jnp.bfloat16),
            dma((7,)),
            dma,
            dma((rest, units + len(Z_UNITS))),
            dma((rest, units)),
            dma((rest, units)),
            dma((rest,)),
            dma((groups,)),
            dma((groups,)),
            dma((groups,)),
        ],
        compiler_params=pltpu.CompilerParams(
            collective_id=0, has_side_effects=True, vmem_limit_bytes=VMEM_KIB * 1024
        ),
        name="tower",
    )(*[
        pltpu.with_memory_space_constraint(x, pltpu.HBM)
        for x in (pooled, cotangent, w_first, w_second, b_first.reshape(1, inner), counts, row_ids)
    ])
    new_accum = accum + summed * summed
    return table - learn_rate * summed / (jnp.sqrt(new_accum) + epsilon), new_accum


def solution(mesh):
    in_specs = (
        P(("wide", "narrow"), None),
        P(("wide", "narrow"), None),
        P("narrow", None),
        P(),
        P("narrow", None),
        P(None, "narrow", "wide"),
        P(None, "narrow"),
        P(None, "narrow", None),
        P(None, "narrow", None),
    )
    out_specs = (P(None, "narrow", None), P(None, "narrow", None))
    step = functools.partial(shards, mesh.shape["wide"], mesh.shape["narrow"])
    return jax.shard_map(step, mesh=mesh, in_specs=in_specs, out_specs=out_specs, check_vma=False)
```

```python
import functools
import math

import jax
import jax.numpy as jnp
from jax import lax
from jax.experimental import pallas as pl
from jax.experimental.pallas import tpu as pltpu
from jax.sharding import PartitionSpec as P

MESH = pl.DeviceIdType.MESH
clip_factor = 0.5
learn_rate = 0.05
epsilon = 1e-08
NT = (((1,), (1,)), ((), ()))
HOP_Z = 3.0
STEP_Z = 0.35 / 2
SPLIT = 2
PACE = 0.0
HOP_S = 3.4
HOP_D = 3.4
HOP_C = 1.4
HOP_W = 3.4
STRAIGHT = 1
END_2 = 0.0
END_3 = 0.0
MID_0 = 0.0
MID_1 = -2.0
MID_2 = 0.0
ACT_TILE = 1024
Z_UNITS = (5,)
HALVES = 2
VMEM_KIB = 32 * 1024


def flip(index, mask):
    bit = 1
    while bit <= mask:
        if mask & bit:
            index = index + bit * (1 - 2 * ((index // bit) % 2))
        bit *= 2
    return index


def pieces_of(shard_rows, n_wide):
    pieces = 1
    while pieces < 8 and n_wide % (2 * pieces) == 0 and shard_rows % (32 * pieces) == 0:
        pieces *= 2
    return pieces


def arrivals(n, n_narrow, count):
    items = []
    for s in range(n_narrow):
        if s != n:
            for v in range(count):
                items.append(((abs(s - n) - 1) * count + v, s > n, s, v))
    return [(s, v) for _, _, s, v in sorted(items)]


def tower_kernel(
    n_wide, n_narrow, pieces, scale, limit,
    pooled_hbm, cot_hbm, w1_hbm, w2_hbm, bias_hbm, counts_hbm, ids_hbm, out_ref,
    pooled, cot, weights, bias, ids, looks, hidden, back, deltas, grad_in, gfull, gsend, grecv, sums,
    local_sem, send_sem, z_sem, side_sem, d_sem, c_sem, look_sem, grad_sem, sum_sem,
):
    wide = lax.axis_index("wide")
    narrow = lax.axis_index("narrow")
    shard, inner = w1_hbm.shape
    top = w2_hbm.shape[1]
    width = top // SPLIT
    units = (inner + top) // width
    piece_rows = shard // pieces
    bags = pooled.shape[0]
    emb = gfull.shape[3]
    tables, slots = looks.shape[1], looks.shape[2]
    rest = n_narrow - 1
    part = wide % pieces
    base = wide - part
    has_core, has_x, has_y = pieces >= 2, pieces >= 4, pieces >= 8
    def lane_block(index, size):
        return pl.ds(pl.multiple_of(index * size, size), size)

    def local(step, src, dst):
        return pltpu.make_async_copy(src, dst, local_sem.at[step])

    own_rows = lane_block(narrow, shard)
    own_w = [
        local(0, w1_hbm, weights.at[own_rows, pl.ds(0, inner)]),
        local(1, w2_hbm, weights.at[own_rows, pl.ds(inner, top)]),
    ]
    own_x = [local(2, pooled_hbm, pooled), local(3, cot_hbm, cot)]
    own_rest = [
        local(4, counts_hbm.at[:, :, lane_block(narrow, bags)], looks.at[narrow]),
        local(5, bias_hbm, bias),
        local(6, ids_hbm, ids),
    ]
    for copy in own_w + own_x + own_rest:
        copy.start()

    barrier = pltpu.get_barrier_semaphore()

    def greet(device):
        pl.semaphore_signal(barrier, inc=1, device_id=device, device_id_type=MESH)

    @pl.when(narrow > 0)
    def _():
        greet({"narrow": narrow - 1})

    @pl.when(narrow < n_narrow - 1)
    def _():
        greet({"narrow": narrow + 1})

    if pieces == n_wide:
        beside = [base + flip(part, m) for m in (1, 2, 4) if m < pieces]
    else:
        beside = [(wide + d) % n_wide for d in range(1, n_wide)]
    for device in beside:
        greet({"wide": device})
    ends = jnp.where(narrow > 0, 1, 0) + jnp.where(narrow < n_narrow - 1, 1, 0)
    pl.semaphore_wait(barrier, ends + len(beside))

    def remote(src, dst, recv, device):
        return pltpu.make_async_remote_copy(
            src_ref=src, dst_ref=dst, send_sem=send_sem, recv_sem=recv,
            device_id=device, device_id_type=MESH,
        )

    sent = []

    def launch(copy, cond=None):
        if cond is None:
            copy.start()
        else:
            @pl.when(cond)
            def _():
                copy.start()
        sent.append((copy, cond))

    def pick(values):
        if all(v == values[0] for v in values):
            return values[0]
        total = 0
        for n, v in enumerate(values):
            total = total + jnp.where(narrow == n, v, 0)
        return total

    def slot_of(s, n):
        return (s - n + n_narrow) % n_narrow - 1

    def view(s, q, u):
        rows = pl.ds(pl.multiple_of(s * shard + q * piece_rows, piece_rows), piece_rows)
        return weights.at[rows, lane_block(u, width)]

    crosses = [u for u in range(units) if has_y and n_narrow <= 4 and u in Z_UNITS]

    def piece_of(s, v):
        if crosses and v >= units:
            return view(s, flip(part, 6), crosses[v - units])
        return view(s, part, v)

    for copy in own_w:
        copy.wait()
    for v in range(units + len(crosses)):
        w = piece_of(narrow, v)
        for ahead, cond in ((narrow + 1, narrow < n_narrow - 1), (narrow - 1, narrow > 0)):
            launch(remote(w, w, z_sem.at[slot_of(narrow, ahead), v], {"narrow": ahead}), cond)

    order = [arrivals(n, n_narrow, units + len(crosses)) for n in range(n_narrow)]
    groups = tables // 2
    ranks = [sorted((s for s in range(n_narrow) if s != n), key=lambda s: (abs(s - n), s > n)) for n in range(n_narrow)]

    def await_view(w, sem):
        remote(w, w, sem, {"narrow": (narrow + 1) % n_narrow}).wait_recv()

    class Role:
        def __init__(self, members):
            self.members = members
            self.started = 0
            self.looks = 0

        def item(self, j):
            pairs = [order[n][j] if n in self.members else (-1, -1) for n in range(n_narrow)]
            fill = order[self.members[0]][j]
            pairs = [fill if p[0] < 0 else p for p in pairs]
            s, u = pick([p[0] for p in pairs]), pick([p[1] for p in pairs])
            assert not crosses or isinstance(u, int)
            return s, u, slot_of(s, narrow)

        def send(self, w, sem, device):
            remote(w, w, sem, device).start()
            self.started += 1

        def straight(self, j):
            return has_y and all(order[n][j][0] in ranks[n][rest - STRAIGHT:] for n in self.members) and (
                not crosses or order[self.members[0]][j][1] not in crosses
            )

        def to_core(self, w, slot):
            if has_core:
                self.send(w, c_sem.at[slot], {"wide": base + flip(part, 1)})

        def chain(self, j):
            s, u, slot = self.item(j)
            w = piece_of(s, u)
            await_view(w, z_sem.at[slot, u])
            if 0 not in self.members:
                ahead = jnp.where(s < narrow, narrow + 1, narrow - 1)
                self.send(w, z_sem.at[slot_of(s, ahead), u], {"narrow": ahead})
            if crosses and u >= units:
                self.to_core(w, slot)

        def plane(self, j):
            s, u, slot = self.item(j)
            w = view(s, part, u)
            if has_x:
                self.send(w, side_sem.at[slot, u], {"wide": base + flip(part, 2)})
            if has_y:
                self.send(w, side_sem.at[slot, u], {"wide": base + flip(part, 4)})
            if self.straight(j):
                self.send(w, d_sem.at[slot, u], {"wide": base + flip(part, 6)})
            self.to_core(w, slot)

        def side(self, j):
            s, u, slot = self.item(j)
            odd = (s + u if crosses else u + jnp.where(u == units - 1, s, 0)) % 2
            beside = 2 if has_y else 1
            await_view(weights.at[pl.ds(0, beside * piece_rows), lane_block(u, width)], side_sem.at[slot, u])
            for mask, there, turn in ((2, 4, 0), (4, 2, 1)):
                if mask < pieces:
                    w = view(s, flip(part, mask), u)
                    if has_y and not (crosses and u in crosses) and not self.straight(j):
                        onward = remote(w, w, d_sem.at[slot, u], {"wide": base + flip(part, there)})

                        @pl.when(odd == turn)
                        def _():
                            onward.start()
                    self.to_core(w, slot)
            if has_y and not (crosses and u in crosses) and not self.straight(j):
                self.started += 1

        def corner(self, j):
            s, u, slot = self.item(j)
            w = view(s, flip(part, 6), u)
            await_view(w, d_sem.at[slot, u])
            self.to_core(w, slot)

        def gathered(self, i):
            s = pick([ranks[n][i] if n in self.members else ranks[self.members[0]][i] for n in range(n_narrow)])
            if has_core:
                await_view(weights.at[pl.ds(0, shard // 2), :], c_sem.at[slot_of(s, narrow)])
            if chunked and i < rest - 1:
                add_chunk(s, False)

        def lookups(self, way):
            d, inner = way
            middle = narrow < n_narrow - 1 - narrow
            up = middle if inner else jnp.logical_not(middle)
            owner = jnp.where(up, narrow + d, narrow - d)
            valid = jnp.logical_and(owner >= 0, owner < n_narrow)
            owner = jnp.where(valid, owner, (narrow + 1) % n_narrow)
            for g in range(groups):
                block = pl.ds(2 * g, 2)
                copy = remote(
                    counts_hbm.at[block, :, lane_block(owner, bags)], looks.at[narrow, block],
                    look_sem.at[g], {"narrow": owner},
                )

                @pl.when(valid)
                def _():
                    copy.start()

        def settle(self):
            most = weights.shape[0] // piece_rows
            count = self.started
            while count > 0:
                k = min(count, most)
                w = weights.at[pl.ds(0, k * piece_rows), pl.ds(0, width)]
                remote(w, w, c_sem.at[0], {"narrow": (narrow + 1) % n_narrow}).wait_send()
                count -= k

    def add_chunk(source, fresh):
        rows = lane_block(source, shard)
        value = jnp.dot(
            pooled[:, rows], weights[rows, pl.ds(0, inner)], preferred_element_type=jnp.float32
        )
        if fresh:
            hidden[...] = value
        else:
            hidden[...] = hidden[...] + value
        back[:, rows] = lax.dot_general(
            cot[...], weights[rows, pl.ds(inner, top)], NT, preferred_element_type=jnp.float32
        )

    chunked = shard % 128 == 0
    for copy in own_x:
        copy.wait()
    if chunked:
        add_chunk(narrow, True)

    roles = [Role([n for n in (0, n_narrow - 1)])]
    if n_narrow > 2:
        roles.append(Role(list(range(1, n_narrow - 1))))
    for r, role in enumerate(roles):
        n = role.members[0]
        plan = []
        at = {}
        placed = 0
        for j, (s, u) in enumerate(order[n]):
            z = HOP_Z * abs(s - n) + STEP_Z * u
            plan.append((z, 0, role.chain, j))
            last = z
            if u < units:
                p = z if r == 0 else max(z, HOP_Z + PACE * placed)
                if role.straight(j):
                    p = max(p, HOP_Z + HOP_S + 0.01)
                placed += 1
                plan.append((p, 1, role.plane, j))
                last = p
                if has_x:
                    last = p + HOP_S
                    plan.append((last, 2, role.side, j))
                if has_y and u not in crosses:
                    last = p + (HOP_W if role.straight(j) else HOP_S + HOP_D)
                    plan.append((last, 3, role.corner, j))
            at[s] = max(last, at.get(s, 0.0))
        done = max(t for t, _, kind, _ in plan if kind == role.chain)
        for d in range(1, n_narrow):
            if r == 0:
                plan.append((0.0 if d == 1 else done + (END_2 if d == 2 else END_3), 1.5, role.lookups, (d, True)))
            else:
                plan.append((done + (MID_1 if d == 1 else MID_2), 1.5, role.lookups, (d, True)))
                plan.append((done + MID_0, 1.5, role.lookups, (d, False)))
        for i in range(rest):
            s = ranks[n][i]
            plan.append((at[s] + HOP_C, 4, role.gathered, i))
        plan.sort(key=lambda e: e[:2])
        kinds = [(e[2], e[3]) for e in plan]
        for j in range(len(order[n])):
            if order[n][j][1] < units and role.straight(j):
                assert kinds.index((role.side, 0)) < kinds.index((role.plane, j))

        @pl.when(jnp.logical_or(narrow == 0, narrow == n_narrow - 1) if r == 0 else jnp.logical_and(narrow > 0, narrow < n_narrow - 1))
        def _():
            for _, _, event, j in plan:
                event(j)

    for copy in own_rest:
        copy.wait()
    tile = min(ACT_TILE, inner)
    if chunked:
        last = lane_block(pick([r[rest - 1] for r in ranks]), shard)
        back[:, last] = lax.dot_general(
            cot[...], weights[last, pl.ds(inner, top)], NT, preferred_element_type=jnp.float32
        )
    for t in range(inner // tile):
        columns = pl.ds(t * tile, tile)
        if chunked:
            value = hidden[:, columns] + jnp.dot(
                pooled[:, last], weights[last, columns], preferred_element_type=jnp.float32
            )
            back_value = back[:, columns]
        else:
            value = jnp.dot(pooled[...], weights[:, columns], preferred_element_type=jnp.float32)
            back_value = lax.dot_general(
                cot[...], weights[columns, pl.ds(inner, top)], NT, preferred_element_type=jnp.float32
            )
        value = value + bias[:, columns]
        sig = jax.nn.sigmoid(value)
        slopes = sig * (1.0 + value * (1.0 - sig))
        deltas[:, columns] = (back_value * slopes).astype(jnp.bfloat16)
    far = [[s for _, s in sorted((-abs(s - n), s) for s in range(n_narrow) if s != n)] for n in range(n_narrow)]
    per_half = groups // HALVES if groups % HALVES == 0 else groups
    for h in range(groups // per_half):
        span = pl.ds(2 * h * per_half * emb, 2 * per_half * emb)
        grad_in[:, span] = lax.dot_general(
            deltas[...], weights[span, pl.ds(0, inner)], NT, preferred_element_type=jnp.float32
        ).astype(jnp.bfloat16)
        for g in range(h * per_half, (h + 1) * per_half):
            await_view(looks.at[pl.ds(0, rest), pl.ds(2 * g, 2)], look_sem.at[g])
        for g in range(h * per_half, (h + 1) * per_half):
            lookups = looks[:, 2 * g:2 * (g + 1)].reshape(n_narrow * 2 * slots, bags)
            value = jnp.dot(
                lookups, grad_in[:, 2 * g * emb:2 * (g + 1) * emb],
                preferred_element_type=jnp.float32,
            )
            value = value.reshape(n_narrow, 2, slots, 2 * emb)
            for i in range(2):
                rows = value[:, i, :, i * emb:(i + 1) * emb]
                gfull[:, 2 * g + i] = rows
                gsend[:, 2 * g + i] = rows.astype(jnp.bfloat16)
        for g in range(h * per_half, (h + 1) * per_half):
            block = pl.ds(2 * g, 2)
            for i in range(rest):
                owner = pick([f[i] for f in far])
                launch(remote(
                    gsend.at[owner, block], grecv.at[slot_of(narrow, owner), block],
                    grad_sem.at[g], {"narrow": owner},
                ))
    for g in range(groups):
        block = pl.ds(2 * g, 2)
        await_view(grecv.at[:, block], grad_sem.at[g])
        total = gfull[narrow, block]
        for d in range(rest):
            total = total + grecv[d, block].astype(jnp.float32)
        grads = total * scale
        norms = jnp.sqrt(jnp.sum(grads * grads, axis=-1, keepdims=True))
        sums[wide, block] = (grads * (limit / jnp.maximum(norms, limit))).astype(jnp.bfloat16)
        for e in range(n_wide - 1, 0, -1):
            peer = base + flip(part, e) if pieces == n_wide else (wide + e) % n_wide
            launch(remote(
                sums.at[wide, block], sums.at[wide, block], sum_sem.at[g], {"wide": peer},
            ))
    for g in range(groups):
        block = pl.ds(2 * g, 2)
        await_view(sums.at[pl.ds(0, n_wide - 1), block], sum_sem.at[g])
        summed = sums[0, block].astype(jnp.float32)
        for q in range(1, n_wide):
            summed = summed + sums[q, block].astype(jnp.float32)
        for i in range(2):
            k = 2 * g + i
            hot = lax.broadcasted_iota(jnp.int32, (out_ref.shape[1], slots), 0) == ids[k:k + 1, :]
            out_ref[k] = jnp.dot(
                hot.astype(jnp.float32), summed[i], precision=lax.Precision.HIGHEST,
                preferred_element_type=jnp.float32,
            )
    for g in range(groups):
        w = looks.at[pl.ds(0, rest), pl.ds(2 * g, 2)]
        remote(w, w, c_sem.at[0], {"narrow": (narrow + 1) % n_narrow}).wait_send()
    for r, role in enumerate(roles):
        @pl.when(jnp.logical_or(narrow == 0, narrow == n_narrow - 1) if r == 0 else jnp.logical_and(narrow > 0, narrow < n_narrow - 1))
        def _():
            role.settle()
    for copy, cond in sent:
        if cond is None:
            copy.wait_send()
        else:
            @pl.when(cond)
            def _():
                copy.wait_send()


def shards(n_wide, n_narrow, pooled, cotangent, w_first, b_first, w_second, counts, row_ids, table, accum):
    tables, slots, group_bags = counts.shape
    emb = table.shape[2]
    bags, emb_all = pooled.shape
    shard, inner = w_first.shape
    top = w_second.shape[1]
    width = top // SPLIT
    units = (inner + top) // width
    pieces = pieces_of(shard, n_wide)
    rest = n_narrow - 1
    groups = tables // 2
    scale = 1.0 / math.sqrt(group_bags)
    limit = clip_factor * math.sqrt(emb)
    hbm = pl.BlockSpec(memory_space=pl.ANY)
    vmem = pl.BlockSpec(memory_space=pltpu.VMEM)
    dma = pltpu.SemaphoreType.DMA
    summed = pl.pallas_call(
        functools.partial(tower_kernel, n_wide, n_narrow, pieces, scale, limit),
        out_shape=jax.ShapeDtypeStruct(table.shape, jnp.float32),
        in_specs=[hbm] * 7,
        out_specs=vmem,
        scratch_shapes=[
            pltpu.VMEM((bags, emb_all), jnp.bfloat16),
            pltpu.VMEM((bags, top), jnp.bfloat16),
            pltpu.VMEM((emb_all, inner + top), jnp.bfloat16),
            pltpu.VMEM((1, inner), jnp.float32),
            pltpu.VMEM(row_ids.shape, jnp.int32),
            pltpu.VMEM((n_narrow, tables, slots, bags), jnp.bfloat16),
            pltpu.VMEM((bags, inner), jnp.float32),
            pltpu.VMEM((bags, inner), jnp.float32),
            pltpu.VMEM((bags, inner), jnp.bfloat16),
            pltpu.VMEM((bags, emb_all), jnp.bfloat16),
            pltpu.VMEM((n_narrow, tables, slots, emb), jnp.float32),
            pltpu.VMEM((n_narrow, tables, slots, emb), jnp.bfloat16),
            pltpu.VMEM((rest, tables, slots, emb), jnp.bfloat16),
            pltpu.VMEM((n_wide, tables, slots, emb), jnp.bfloat16),
            dma((7,)),
            dma,
            dma((rest, units + len(Z_UNITS))),
            dma((rest, units)),
            dma((rest, units)),
            dma((rest,)),
            dma((groups,)),
            dma((groups,)),
            dma((groups,)),
        ],
        compiler_params=pltpu.CompilerParams(
            collective_id=0, has_side_effects=True, vmem_limit_bytes=VMEM_KIB * 1024
        ),
        name="tower",
    )(*[
        pltpu.with_memory_space_constraint(x, pltpu.HBM)
        for x in (pooled, cotangent, w_first, w_second, b_first.reshape(1, inner), counts, row_ids)
    ])
    new_accum = accum + summed * summed
    return table - learn_rate * summed / (jnp.sqrt(new_accum) + epsilon), new_accum


def solution(mesh):
    in_specs = (
        P(("wide", "narrow"), None),
        P(("wide", "narrow"), None),
        P("narrow", None),
        P(),
        P("narrow", None),
        P(None, "narrow", "wide"),
        P(None, "narrow"),
        P(None, "narrow", None),
        P(None, "narrow", None),
    )
    out_specs = (P(None, "narrow", None), P(None, "narrow", None))
    step = functools.partial(shards, mesh.shape["wide"], mesh.shape["narrow"])
    return jax.shard_map(step, mesh=mesh, in_specs=in_specs, out_specs=out_specs, check_vma=False)
```
